32 devices in a mesh: beam: 2 (over x), freq: 16 (over z, y, core).
Axes of the slice: x: 2, y: 2, z: 4, core: 2. Of those that a mesh axis runs over, the one named last changes fastest.
Arguments:
- spectrum: bfloat16 [2, 65536], P(None, ('beam', 'freq')), parts along dimension 1, may hold values from -6 to 6
- template_bank: bfloat16 [2, 256, 1024], replicated, may hold values from -0.125 to 0.125
- template_index: int32 [128], replicated, may hold values from 0 to 255
Outputs:
- harmonic_sum: float32 [128, 65536], P(None, ('beam', 'freq')), parts along dimension 1
The draws below stay inside these ranges and needn't reach their ends.
There are 2 independent parts, one for each index of `beam`. The reference program is written for one: setup_inputs(seed, part) draws one part's arguments, and reference() takes and returns one part's arrays. A program takes and returns all parts, laid end to end along the dimension named above; an argument that names none is the same for every part. Nothing has to cross between parts.
Inputs may be any that keep to these rules, and one draw needn't show every extreme that they name: `template_index`: entry z names the bank template of acceleration row z.
All inputs are finite; a program needn't handle non-finite values.
Results may differ from the reference program's by a relative error of at most 0.002.
Values may be sent and summed in bfloat16 or wider, within the bound.
A program may use at most 64 MiB of HBM per device.

```python
import jax
import jax.numpy as jnp
from jax import lax

ZROWS = 128
TAPS = 1024
NBANK = 256
BINS = 32768


def set_ends(array, stream_key, smallest, largest):
    shape = array.shape
    spot = [jax.random.randint(jax.random.fold_in(stream_key, axis), (), 0, shape[axis]) for axis in range(len(shape))]
    array = array.at[tuple(spot)].set(smallest)
    longest = shape.index(max(shape))
    spot[longest] = (spot[longest] + 1) % shape[longest]
    return array.at[tuple(spot)].set(largest)


def shard_levels(rng, shape, pieces, low, high):
    factor_of, own = 1.0, jax.random.fold_in(rng, 6)
    for dim, shards_of in pieces:
        draws = jnp.exp(jax.random.uniform(jax.random.fold_in(own, dim), (shards_of,), jnp.float32, low / len(pieces), high / len(pieces)))
        factor_of = factor_of * jnp.repeat(draws, shape[dim] // shards_of).reshape([-1 if axis == dim else 1 for axis in range(len(shape))])
    return factor_of


def bell_draw(stream_key, shape, spread, limit, cuts=(), kind=jnp.bfloat16):
    values = spread * jax.random.normal(stream_key, shape, jnp.float32)
    if cuts:
        values = values * shard_levels(stream_key, shape, cuts, -0.22, 0.18)
    return jnp.clip(values, -limit, limit).astype(kind)


def setup_inputs(seed: int = 0, part: int = 0) -> dict:
    key_of = jax.random.split(jax.random.key(seed), 4)
    part_splits = jax.random.split(jax.random.fold_in(key_of[3], part), 4)
    return {
        "spectrum": bell_draw(part_splits[0], (2, BINS), 1.0, 6.0, ((1, 16),)),
        "template_bank": bell_draw(key_of[1], (2, NBANK, TAPS), (2 * TAPS) ** -0.5, 0.125),
        "template_index": set_ends(jax.random.randint(key_of[2], (ZROWS,), 0, NBANK), jax.random.fold_in(key_of[2], 1), 0, NBANK - 1).astype(jnp.int32),
    }


def reference(spectrum, template_bank, template_index):
    half_taps = TAPS // 2
    length_fft = 2 * BINS
    template_re = template_bank[0][template_index].astype(jnp.float32)
    template_im = template_bank[1][template_index].astype(jnp.float32)
    signal = lax.complex(spectrum[0].astype(jnp.float32), spectrum[1].astype(jnp.float32))
    padded = jnp.pad(signal, (half_taps, length_fft - BINS - half_taps))
    signal_freq = jnp.fft.fft(padded)

    def correlate_row(pair):
        row_re, row_im = pair
        row = lax.complex(row_re, row_im)
        row_pad = jnp.pad(row, (0, length_fft - TAPS))
        kernel_freq = jnp.conj(jnp.fft.fft(jnp.conj(row_pad)))
        correlated = jnp.fft.ifft(signal_freq * kernel_freq)[:BINS]
        real_part = jnp.real(correlated)
        imag_part = jnp.imag(correlated)
        return (real_part * real_part + imag_part * imag_part).astype(jnp.bfloat16)

    plane = lax.map(correlate_row, (template_re, template_im))
    total = plane.astype(jnp.float32)
    for numerator, denominator in ((1, 2), (1, 4), (3, 4)):
        row_index = (jnp.arange(ZROWS, dtype=jnp.int32) * numerator) // denominator
        col_index = (jnp.arange(BINS, dtype=jnp.int32) * numerator) // denominator
        total = total + plane[row_index][:, col_index].astype(jnp.float32)
    return total
```

```python
import functools
import math

import jax
import jax.numpy as jnp
from jax import lax
from jax.experimental import pallas as pl
from jax.experimental.pallas import tpu as pltpu
from jax.sharding import PartitionSpec as P

RATIOS = ((1, 1), (1, 2), (1, 4), (3, 4))
CHUNK = 256
LANES = 128
TILE = 16


class Piece:
    def __init__(self, part, period, residue, offset, peers, begin, count, place):
        self.part, self.period, self.residue, self.offset, self.peers = part, period, residue, offset, peers
        self.begin, self.count, self.place = begin, count, place

    def peer(self, me):
        return (me // self.period) * self.peers + self.offset

    def holds(self, me, owners):
        peer = self.peer(me)
        fits = (peer >= 0) & (peer < owners)
        if self.period > 1:
            fits = fits & (lax.rem(me, self.period) == self.residue)
        return fits


class Plan:
    def __init__(self, cols, taps, rows, owners):
        self.cols, self.taps, self.rows, self.owners = cols, taps, rows, owners
        self.granule = taps // 2
        self.held = cols // self.granule
        self.steps = [self.held * n // d for n, d in RATIOS]
        self.part_cols = [cols * n // d for n, d in RATIOS]
        self.part_rows = [rows * n // d for n, d in RATIOS]
        self.reach = max(1, 6 * owners // 16)
        self.sends, self.receives, self.bases = [], [], []
        slots = 0
        for part, step in enumerate(self.steps):
            self.bases.append(slots)
            slots += step + 2
            common = math.gcd(step, self.held)
            sources, targets = step // common, self.held // common
            for source in range(sources):
                for target in range(-targets - 2, 2 * targets + 3):
                    self.add(self.sends, part, sources, targets, source, target, True)
            for target in range(targets):
                for source in range(-sources - 2, 2 * sources + 3):
                    self.add(self.receives, part, sources, targets, source, target, False)
        self.slots = slots

    def add(self, pieces, part, sources, targets, source, target, sending):
        if part == 0 and source == target:
            return
        step = self.steps[part]
        first = step * target - 1
        low = max(self.held * source, first)
        high = min(self.held * (source + 1), first + step + 2)
        if low < high:
            order = (sources, source, target, targets) if sending else (targets, target, source, sources)
            pieces.append(Piece(part, *order, low - self.held * source, high - low, low - first))

    def far(self, source, target):
        return target - source >= self.reach


def one_hot(shape, make):
    left = lax.broadcasted_iota(jnp.int32, shape, 0)
    right = lax.broadcasted_iota(jnp.int32, shape, 1)
    return make(left, right).astype(jnp.float32).astype(jnp.bfloat16)


def build(window, shifts, low, high):
    width = (high - low + 1) * LANES
    start = low * LANES
    for which in (0, 1):
        line = window[which : which + 1, start : start + width].astype(jnp.float32)
        base = jnp.broadcast_to(line, (8, width))
        place = lax.broadcasted_iota(jnp.int32, (8, width), 0)
        for bit in (1, 2, 4):
            base = jnp.where((place & bit) != 0, pltpu.roll(base, width - bit, 1), base)
        base = jnp.concatenate([base, pltpu.roll(base, width - 8, 1)], 0).astype(jnp.bfloat16)
        for turn in range(LANES // TILE):
            moved = base if turn == 0 else pltpu.roll(base, width - TILE * turn, 1)
            for block in range(high - low):
                spot = (low + block) * LANES + TILE * turn
                shifts[which][spot : spot + TILE, :] = moved[:, block * LANES : (block + 1) * LANES]


def power(lhs, shifts, count, taps, start):
    rows = lhs.shape[1] // 2
    slabs = range(lhs.shape[0])
    if count == rows:
        left = jnp.concatenate([lhs[slab] for slab in slabs], 1)
    else:
        left = jnp.concatenate(
            [jnp.concatenate([lhs[slab, :count], lhs[slab, rows : rows + count]], 0) for slab in slabs], 1
        )
    right = jnp.concatenate(
        [
            jnp.concatenate([shifts[which][start + at : start + at + taps, :] for at in range(0, CHUNK, LANES)], 1)
            for which in (0, 1)
        ],
        0,
    )
    both = jnp.dot(left, right, preferred_element_type=jnp.float32)
    real, imag = both[:count], both[count:]
    return (real * real + imag * imag).astype(jnp.bfloat16)


def planes_kernel(plan, spec_ref, index_ref, bank_ref, *refs):
    parts = len(RATIOS)
    planes, wins = refs[:parts], refs[parts : 2 * parts]
    shifts = [refs[2 * parts + 2 * part : 2 * parts + 2 * part + 2] for part in range(parts)]
    bank, index, lhs, in_sems, send_sems, recv_sems, ready = refs[4 * parts :]
    rows, taps, size, cols, owners = plan.rows, plan.taps, plan.granule, plan.cols, plan.owners
    me = lax.axis_index("freq")
    win = wins[0]

    fetch_own = pltpu.make_async_copy(spec_ref, win.at[:, size : size + cols], in_sems.at[0])
    fetch_own.start()
    fetch_index = pltpu.make_async_copy(index_ref, index, in_sems.at[1])
    fetch_index.start()
    fetch_bank = pltpu.make_async_copy(bank_ref, bank, in_sems.at[2])
    fetch_bank.start()

    barrier = pltpu.get_barrier_semaphore()

    def signal(semaphore, peer):
        pl.semaphore_signal(semaphore, inc=1, device_id={"freq": peer}, device_id_type=pl.DeviceIdType.MESH)

    def remote(piece):
        return piece.holds(me, owners) & (piece.peer(me) != me)

    def far_receive(piece):
        return plan.far(piece.peer(me), me)

    def far_send(piece):
        return plan.far(me, piece.peer(me))

    expected = jnp.int32(0)
    late = jnp.int32(0)
    for piece in plan.receives:
        pl.when(remote(piece) & jnp.logical_not(far_receive(piece)))(
            functools.partial(signal, barrier, piece.peer(me))
        )
        expected += jnp.where(remote(piece) & far_receive(piece), 1, 0)
    for piece in plan.sends:
        pl.when(remote(piece) & far_send(piece))(functools.partial(signal, barrier, piece.peer(me)))
        expected += jnp.where(remote(piece) & jnp.logical_not(far_send(piece)), 1, 0)
        late += jnp.where(remote(piece) & far_send(piece), 1, 0)

    @pl.when(me == 0)
    def _():
        for part in range(parts):
            wins[part][:, 0:size] = jnp.zeros((2, size), win.dtype)

    @pl.when(me == owners - 1)
    def _():
        win[:, size + cols :] = jnp.zeros((2, size), win.dtype)

    def spots(piece):
        source = win.at[:, size * (1 + piece.begin) : size * (1 + piece.begin + piece.count)]
        target = wins[piece.part].at[:, size * piece.place : size * (piece.place + piece.count)]
        return source, target, recv_sems.at[plan.bases[piece.part] + piece.place]

    def copy_of(number, piece):
        source, target, got = spots(piece)
        return pltpu.make_async_remote_copy(
            src_ref=source,
            dst_ref=target,
            send_sem=send_sems.at[number],
            recv_sem=got,
            device_id={"freq": piece.peer(me)},
            device_id_type=pl.DeviceIdType.MESH,
        )

    def send(far):
        for number, piece in enumerate(plan.sends):
            chosen = far_send(piece) if far else jnp.logical_not(far_send(piece))
            pl.when(remote(piece) & chosen)(lambda number=number, piece=piece: copy_of(number, piece).start())

    def receive(part):
        for piece in plan.receives:
            if piece.part == part:
                source, target, got = spots(piece)
                landed = win.at[:, size : size * (1 + piece.count)]
                pl.when(piece.holds(me, owners))(
                    lambda landed=landed, target=target, got=got: pltpu.make_async_copy(landed, target, got).wait()
                )

    blocks = [(width + taps) // LANES - 1 for width in plan.part_cols]
    halo = size // LANES
    edge = size // CHUNK
    chunks = cols // CHUNK

    def keep(part, chunk):
        planes[part][:, chunk * CHUNK : (chunk + 1) * CHUNK] = power(
            lhs, shifts[part], plan.part_rows[part], taps, chunk * CHUNK
        )

    fetch_own.wait()
    for piece in plan.sends:
        if piece.part:
            source, target, got = spots(piece)
            pl.when(piece.holds(me, owners) & (piece.peer(me) == me))(
                lambda source=source, target=target, got=got: pltpu.make_async_copy(source, target, got).start()
            )
    pl.when(expected > 0)(lambda: pl.semaphore_wait(barrier, expected))
    send(False)
    for piece in plan.receives:
        pl.when(remote(piece) & far_receive(piece))(functools.partial(signal, ready, piece.peer(me)))
    build(win, shifts[0], halo, blocks[0] - halo)
    fetch_index.wait()
    fetch_bank.wait()
    names = lax.broadcasted_iota(jnp.int32, (bank.shape[1], rows), 0)
    picks = (names == index[...]).astype(jnp.float32).T.astype(jnp.bfloat16)
    real = jnp.dot(picks, bank[0], preferred_element_type=jnp.float32).astype(jnp.bfloat16)
    imag = jnp.dot(picks, bank[1], preferred_element_type=jnp.float32).astype(jnp.bfloat16)
    slabs = taps // LANES
    for slab in range(slabs):
        piece = slice(slab * LANES, (slab + 1) * LANES)
        lhs[slab, :rows] = real[:, piece]
        lhs[slab, rows:] = imag[:, piece]
        lhs[slabs + slab, :rows] = -imag[:, piece]
        lhs[slabs + slab, rows:] = real[:, piece]
    for chunk in range(edge, chunks - edge):
        keep(0, chunk)
    receive(0)
    build(win, shifts[0], 0, halo)
    build(win, shifts[0], blocks[0] - halo, blocks[0])
    for chunk in [*range(edge), *range(chunks - edge, chunks)]:
        keep(0, chunk)
    pl.when(late > 0)(lambda: pl.semaphore_wait(ready, late))
    send(True)
    for part in (3, 1, 2):
        receive(part)
        build(wins[part], shifts[part], 0, blocks[part])
        for chunk in range(plan.part_cols[part] // CHUNK):
            keep(part, chunk)
    for number, piece in enumerate(plan.sends):
        pl.when(remote(piece))(lambda number=number, piece=piece: copy_of(number, piece).wait_send())


def sum_kernel(plan, *refs):
    parts = len(RATIOS)
    planes, out_ref, out, sems = refs[:parts], *refs[parts:]
    chunks = plan.cols // CHUNK

    def put(chunk):
        spot = slice(chunk * CHUNK, (chunk + 1) * CHUNK)
        return pltpu.make_async_copy(out.at[:, spot], out_ref.at[:, spot], sems.at[chunk])

    widths = [CHUNK * n // d for n, d in RATIOS]
    depths = [-(-width // LANES) * LANES for width in widths]

    def spread(part, skip):
        n, d = RATIOS[part]
        return one_hot((depths[part], CHUNK), lambda k, r: k == skip + r * n // d)

    count = sum(plan.part_rows[1:])
    below, choose = 0, None
    left = lax.broadcasted_iota(jnp.int32, (plan.rows, count), 0)
    right = lax.broadcasted_iota(jnp.int32, (plan.rows, count), 1)
    for part in range(1, parts):
        n, d = RATIOS[part]
        hit = right == below + left * n // d
        choose = hit if choose is None else choose | hit
        below += plan.part_rows[part]
    choose = choose.astype(jnp.float32).astype(jnp.bfloat16)
    tables = {}
    for chunk in range(chunks):
        cells = []
        for part in range(1, parts):
            start = widths[part] * chunk
            skip = start % LANES
            if (part, skip) not in tables:
                tables[part, skip] = spread(part, skip)
            start -= skip
            lhs = planes[part][:, start : start + depths[part]]
            cells.append(jnp.dot(lhs, tables[part, skip], preferred_element_type=jnp.float32).astype(jnp.bfloat16))
        total = planes[0][:, chunk * CHUNK : (chunk + 1) * CHUNK].astype(jnp.float32)
        total += jnp.dot(choose, jnp.concatenate(cells, 0), preferred_element_type=jnp.float32)
        out[:, chunk * CHUNK : (chunk + 1) * CHUNK] = total
        put(chunk).start()
    for chunk in range(chunks):
        put(chunk).wait()


def body(spectrum, template_bank, template_index):
    owners = lax.axis_size("freq")
    taps = template_bank.shape[2]
    rows = template_index.shape[0]
    cols = spectrum.shape[1]
    plan = Plan(cols, taps, rows, owners)
    parts = len(RATIOS)
    hbm = pl.BlockSpec(memory_space=pltpu.HBM)
    vmem = pl.BlockSpec(memory_space=pltpu.VMEM)
    planes = pl.pallas_call(
        functools.partial(planes_kernel, plan),
        out_shape=tuple(
            pltpu.VMEM((count, width), jnp.bfloat16) for count, width in zip(plan.part_rows, plan.part_cols)
        ),
        in_specs=[hbm] * 3,
        out_specs=(vmem,) * parts,
        scratch_shapes=[
            *[pltpu.VMEM((2, width + taps), jnp.bfloat16) for width in plan.part_cols],
            *[pltpu.VMEM((width + taps, LANES), jnp.bfloat16) for width in plan.part_cols for _ in range(2)],
            pltpu.VMEM(template_bank.shape, jnp.bfloat16),
            pltpu.VMEM((1, rows), jnp.int32),
            pltpu.VMEM((2 * taps // LANES, 2 * rows, LANES), jnp.bfloat16),
            pltpu.SemaphoreType.DMA((3,)),
            pltpu.SemaphoreType.DMA((len(plan.sends),)),
            pltpu.SemaphoreType.DMA((plan.slots,)),
            pltpu.SemaphoreType.REGULAR,
        ],
        compiler_params=pltpu.CompilerParams(collective_id=0, has_side_effects=True, vmem_limit_bytes=24 * 2**20),
        name="planes",
    )(*[pltpu.with_memory_space_constraint(x, pltpu.HBM) for x in (spectrum, template_index.reshape(1, rows), template_bank)])
    return pl.pallas_call(
        functools.partial(sum_kernel, plan),
        out_shape=jax.ShapeDtypeStruct((rows, cols), jnp.float32),
        in_specs=[vmem] * parts,
        out_specs=hbm,
        scratch_shapes=[
            pltpu.VMEM((rows, cols), jnp.float32),
            pltpu.SemaphoreType.DMA((cols // CHUNK,)),
        ],
        compiler_params=pltpu.CompilerParams(vmem_limit_bytes=24 * 2**20),
        name="sums",
    )(*planes)


def solution(mesh):
    return jax.shard_map(
        body,
        mesh=mesh,
        in_specs=(P(None, ("beam", "freq")), P(), P()),
        out_specs=P(None, ("beam", "freq")),
        check_vma=False,
    )
```

```python
import functools

import jax
import jax.numpy as jnp
from jax import lax
from jax.experimental import pallas as pl
from jax.experimental.pallas import tpu as pltpu
from jax.sharding import PartitionSpec as P

RATIOS = ((1, 1), (1, 2), (1, 4), (3, 4))
CHUNK = 256
LANES = 128
TILE = 16


class Plan:
    def __init__(self, cols, taps, rows, owners):
        self.cols, self.taps, self.rows, self.owners = cols, taps, rows, owners
        self.granule = taps // 2
        self.held = cols // self.granule
        self.steps = [self.held * n // d for n, d in RATIOS]
        self.part_cols = [cols * n // d for n, d in RATIOS]
        self.part_rows = [rows * n // d for n, d in RATIOS]
        self.reach = max(2, 6 * owners // 16)
        self.most = max(sum(count for _, _, _, count, _ in self.sends(source)) for source in range(owners))

    def pieces(self, source, target):
        found = []
        for part, step in enumerate(self.steps):
            first = step * target - 1
            low = max(self.held * source, first)
            high = min(self.held * (source + 1), first + step + 2)
            if low < high and (part or source != target):
                found.append((part, target, low - self.held * source, high - low, low - first))
        return found

    def sends(self, source):
        near = range(max(0, source - 1), min(self.owners, 4 * source + 8))
        return [piece for target in near for piece in self.pieces(source, target)]

    def far(self, source, target):
        return target - source >= self.reach

    def targets(self, me, far):
        return [to for to in range(self.owners) if to != me and self.far(me, to) == far and self.pieces(me, to)]

    def sources(self, me, far):
        return [by for by in range(self.owners) if by != me and self.far(by, me) == far and self.pieces(by, me)]


def choose(me, low, high, act):
    if high - low == 1:
        act(low)
    else:
        middle = (low + high) // 2
        pl.when(me < middle)(lambda: choose(me, low, middle, act))
        pl.when(me >= middle)(lambda: choose(me, middle, high, act))


def one_hot(shape, make):
    left = lax.broadcasted_iota(jnp.int32, shape, 0)
    right = lax.broadcasted_iota(jnp.int32, shape, 1)
    return make(left, right).astype(jnp.float32).astype(jnp.bfloat16)


def build(window, shifts, low, high):
    width = (high - low + 1) * LANES
    start = low * LANES
    for which in (0, 1):
        line = window[which : which + 1, start : start + width].astype(jnp.float32)
        base = jnp.broadcast_to(line, (8, width))
        place = lax.broadcasted_iota(jnp.int32, (8, width), 0)
        for bit in (1, 2, 4):
            base = jnp.where((place & bit) != 0, pltpu.roll(base, width - bit, 1), base)
        base = jnp.concatenate([base, pltpu.roll(base, width - 8, 1)], 0).astype(jnp.bfloat16)
        for turn in range(LANES // TILE):
            moved = base if turn == 0 else pltpu.roll(base, width - TILE * turn, 1)
            for block in range(high - low):
                spot = (low + block) * LANES + TILE * turn
                shifts[which][spot : spot + TILE, :] = moved[:, block * LANES : (block + 1) * LANES]


def rows_of(lhs, count, slabs):
    rows = lhs.shape[1] // 2
    if count == rows:
        return jnp.concatenate([lhs[slab] for slab in slabs], 1)
    return jnp.concatenate(
        [jnp.concatenate([lhs[slab, :count], lhs[slab, rows : rows + count]], 0) for slab in slabs], 1
    )


def correlate(lhs, shifts, count, start, tiles):
    half = lhs.shape[0] // 2
    each = CHUNK // LANES
    slabs = [which * half + each * tile + at for which in (0, 1) for tile in tiles for at in range(each)]
    right = jnp.concatenate(
        [
            jnp.concatenate(
                [shifts[which][spot + at : spot + at + CHUNK, :] for at in range(0, CHUNK, LANES)], 1
            )
            for which in (0, 1)
            for spot in [start + CHUNK * tile for tile in tiles]
        ],
        0,
    )
    return jnp.dot(rows_of(lhs, count, slabs), right, preferred_element_type=jnp.float32)


def power(both):
    count = both.shape[0] // 2
    real, imag = both[:count], both[count:]
    return (real * real + imag * imag).astype(jnp.bfloat16)


def planes_kernel(plan, spec_ref, index_ref, bank_ref, plane, plane3, win1, win2, lhs, win, win3, *refs):
    shifts, shifts3 = refs[:2], refs[2:4]
    acc, bank, index, zeros, sized, in_sems, send_sem, recv_sems, ready = refs[4:]
    wins = (win, win1, win2, win3)
    rows, taps, size, cols, owners = plan.rows, plan.taps, plan.granule, plan.cols, plan.owners
    parts = len(RATIOS)
    me = lax.axis_index("freq")

    fetch_own = pltpu.make_async_copy(spec_ref, win.at[:, size : size + cols], in_sems.at[0])
    fetch_own.start()
    fetch_index = pltpu.make_async_copy(index_ref, index, in_sems.at[1])
    fetch_index.start()
    fetch_bank = pltpu.make_async_copy(bank_ref, bank, in_sems.at[2])
    fetch_bank.start()
    barrier = pltpu.get_barrier_semaphore()

    def signal(semaphore, peer):
        pl.semaphore_signal(semaphore, inc=1, device_id={"freq": peer}, device_id_type=pl.DeviceIdType.MESH)

    def greet(k):
        for peer in plan.sources(k, False) + plan.targets(k, True):
            signal(barrier, peer)

    choose(me, 0, owners, greet)
    zeros[...] = jnp.zeros(zeros.shape, zeros.dtype)

    def send(k, far):
        for part, to, begin, count, place in plan.sends(k):
            source = win.at[:, size * (1 + begin) : size * (1 + begin + count)]
            target = wins[part].at[:, size * place : size * (place + count)]
            if to == k:
                if not far:
                    pltpu.make_async_copy(source, target, recv_sems.at[part]).start()
            elif plan.far(k, to) == far:
                pltpu.make_async_remote_copy(
                    src_ref=source,
                    dst_ref=target,
                    send_sem=send_sem,
                    recv_sem=recv_sems.at[part],
                    device_id={"freq": to},
                    device_id_type=pl.DeviceIdType.MESH,
                ).start()

    def fill(part, spot):
        pltpu.make_async_copy(zeros, wins[part].at[:, spot : spot + size], recv_sems.at[part]).start()

    def first(k):
        count = len(plan.targets(k, False)) + len(plan.sources(k, True))
        if count:
            pl.semaphore_wait(barrier, count)
        send(k, False)
        for peer in plan.sources(k, True):
            signal(ready, peer)
        if k == 0:
            for part in range(parts):
                fill(part, 0)
        if k == owners - 1:
            fill(0, size + cols)

    def second(k):
        count = len(plan.targets(k, True))
        if count:
            pl.semaphore_wait(ready, count)
            send(k, True)

    def third(k):
        total = sum(count for _, to, _, count, _ in plan.sends(k) if to != k)
        if total:
            whole = sized.at[:, : total * size]
            pltpu.make_async_copy(whole, whole, send_sem).wait()

    def receive(part):
        whole = sized.at[:, : 2 * size if part == 0 else plan.part_cols[part] + taps]
        pltpu.make_async_copy(whole, whole, recv_sems.at[part]).wait()

    blocks = (cols + taps) // LANES - 1
    halo = size // LANES
    chunks = cols // CHUNK
    tiles = taps // CHUNK
    low, high = size // CHUNK, (size + cols) // CHUNK - 1

    fetch_own.wait()
    choose(me, 0, owners, first)
    build(win, shifts, halo, blocks - halo)
    fetch_index.wait()
    fetch_bank.wait()
    names = lax.broadcasted_iota(jnp.int32, (bank.shape[1], rows), 0)
    picks = (names == index[...]).astype(jnp.float32).T.astype(jnp.bfloat16)
    real = jnp.dot(picks, bank[0], preferred_element_type=jnp.float32).astype(jnp.bfloat16)
    imag = jnp.dot(picks, bank[1], preferred_element_type=jnp.float32).astype(jnp.bfloat16)
    slabs = taps // LANES
    for slab in range(slabs):
        piece = slice(slab * LANES, (slab + 1) * LANES)
        lhs[slab, :rows] = real[:, piece]
        lhs[slab, rows:] = imag[:, piece]
        lhs[slabs + slab, :rows] = -imag[:, piece]
        lhs[slabs + slab, rows:] = real[:, piece]
    edges = []
    for chunk in range(chunks):
        start = chunk * CHUNK
        here = [tile for tile in range(tiles) if low <= chunk + tile < high]
        there = [tile for tile in range(tiles) if tile not in here]
        both = correlate(lhs, shifts, rows, start, here)
        if there:
            acc[len(edges)] = both
            edges.append((start, there))
        else:
            plane[:, start : start + CHUNK] = power(both)
    receive(0)
    build(win, shifts, 0, halo)
    build(win, shifts, blocks - halo, blocks)
    for number, (start, there) in enumerate(edges):
        plane[:, start : start + CHUNK] = power(acc[number] + correlate(lhs, shifts, rows, start, there))
    receive(3)
    build(win3, shifts3, 0, (plan.part_cols[3] + taps) // LANES - 1)
    for start in range(0, plan.part_cols[3], CHUNK):
        plane3[:, start : start + CHUNK] = power(correlate(lhs, shifts3, plan.part_rows[3], start, range(tiles)))
    choose(me, 0, owners, second)
    choose(me, 0, owners, third)
    receive(1)
    receive(2)


def sum_kernel(plan, plane, plane3, win1, win2, lhs, out_ref, out, plane1, plane2, *refs):
    shifts1, shifts2, sems = refs[:2], refs[2:4], refs[4]
    planes = (plane, plane1, plane2, plane3)
    parts = len(RATIOS)
    chunks, taps = plan.cols // CHUNK, plan.taps
    tiles = range(taps // CHUNK)

    def put(chunk):
        spot = slice(chunk * CHUNK, (chunk + 1) * CHUNK)
        return pltpu.make_async_copy(out.at[:, spot], out_ref.at[:, spot], sems.at[chunk])

    widths = [CHUNK * n // d for n, d in RATIOS]
    depths = [-(-width // LANES) * LANES for width in widths]

    def spread(part, skip):
        n, d = RATIOS[part]
        return one_hot((depths[part], CHUNK), lambda k, r: k == skip + r * n // d)

    def fill(part, shifts, start):
        planes[part][:, start : start + CHUNK] = power(correlate(lhs, shifts, plan.part_rows[part], start, tiles))

    build(win2, shifts2, 0, (plan.part_cols[2] + taps) // LANES - 1)
    for start in range(0, plan.part_cols[2], CHUNK):
        fill(2, shifts2, start)
    build(win1, shifts1, 0, (plan.part_cols[1] + taps) // LANES - 1)
    count = sum(plan.part_rows[1:])
    below, pick = 0, None
    left = lax.broadcasted_iota(jnp.int32, (plan.rows, count), 0)
    right = lax.broadcasted_iota(jnp.int32, (plan.rows, count), 1)
    for part in range(1, parts):
        n, d = RATIOS[part]
        hit = right == below + left * n // d
        pick = hit if pick is None else pick | hit
        below += plan.part_rows[part]
    pick = pick.astype(jnp.float32).astype(jnp.bfloat16)
    tables = {}
    for chunk in range(chunks):
        if chunk * widths[1] % CHUNK == 0:
            fill(1, shifts1, chunk * widths[1])
        cells = []
        for part in range(1, parts):
            start = widths[part] * chunk
            skip = start % LANES
            if (part, skip) not in tables:
                tables[part, skip] = spread(part, skip)
            start -= skip
            source = planes[part][:, start : start + depths[part]]
            cells.append(jnp.dot(source, tables[part, skip], preferred_element_type=jnp.float32).astype(jnp.bfloat16))
        total = plane[:, chunk * CHUNK : (chunk + 1) * CHUNK].astype(jnp.float32)
        total += jnp.dot(pick, jnp.concatenate(cells, 0), preferred_element_type=jnp.float32)
        out[:, chunk * CHUNK : (chunk + 1) * CHUNK] = total
        put(chunk).start()
    for chunk in range(chunks):
        put(chunk).wait()


def body(spectrum, template_bank, template_index):
    owners = lax.axis_size("freq")
    taps = template_bank.shape[2]
    rows = template_index.shape[0]
    cols = spectrum.shape[1]
    plan = Plan(cols, taps, rows, owners)
    hbm = pl.BlockSpec(memory_space=pltpu.HBM)
    vmem = pl.BlockSpec(memory_space=pltpu.VMEM)
    wide = [width + taps for width in plan.part_cols]

    def held(*shape, kind=jnp.bfloat16):
        return pltpu.VMEM(shape, kind)

    between = (
        held(rows, cols),
        held(plan.part_rows[3], plan.part_cols[3]),
        held(2, wide[1]),
        held(2, wide[2]),
        held(2 * taps // LANES, 2 * rows, LANES),
    )
    inputs = (spectrum, template_index.reshape(1, rows), template_bank)
    results = pl.pallas_call(
        functools.partial(planes_kernel, plan),
        out_shape=between,
        in_specs=[hbm] * 3,
        out_specs=(vmem,) * len(between),
        scratch_shapes=[
            held(2, wide[0]),
            held(2, wide[3]),
            *[held(wide[part], LANES) for part in (0, 0, 3, 3)],
            held(2 * (taps // 2 // CHUNK), 2 * rows, CHUNK, kind=jnp.float32),
            held(*template_bank.shape),
            held(1, rows, kind=jnp.int32),
            held(2, plan.granule),
            held(2, max(plan.granule * plan.most, *wide)),
            pltpu.SemaphoreType.DMA((3,)),
            pltpu.SemaphoreType.DMA,
            pltpu.SemaphoreType.DMA((len(RATIOS),)),
            pltpu.SemaphoreType.REGULAR,
        ],
        compiler_params=pltpu.CompilerParams(collective_id=0, has_side_effects=True, vmem_limit_bytes=24 * 2**20),
        name="planes",
    )(*[pltpu.with_memory_space_constraint(x, pltpu.HBM) for x in inputs])
    return pl.pallas_call(
        functools.partial(sum_kernel, plan),
        out_shape=jax.ShapeDtypeStruct((rows, cols), jnp.float32),
        in_specs=[vmem] * len(between),
        out_specs=hbm,
        scratch_shapes=[
            held(rows, cols, kind=jnp.float32),
            *[held(plan.part_rows[part], plan.part_cols[part]) for part in (1, 2)],
            *[held(wide[part], LANES) for part in (1, 1, 2, 2)],
            pltpu.SemaphoreType.DMA((cols // CHUNK,)),
        ],
        compiler_params=pltpu.CompilerParams(vmem_limit_bytes=24 * 2**20),
        name="sums",
    )(*results)


def solution(mesh):
    return jax.shard_map(
        body,
        mesh=mesh,
        in_specs=(P(None, ("beam", "freq")), P(), P()),
        out_specs=P(None, ("beam", "freq")),
        check_vma=False,
    )
```

```python
import functools

import jax
import jax.numpy as jnp
from jax import lax
from jax.experimental import pallas as pl
from jax.experimental.pallas import tpu as pltpu
from jax.sharding import PartitionSpec as P

RATIOS = ((1, 1), (1, 2), (1, 4), (3, 4))
CHUNK = 256
LANES = 128
TILE = 16


class Plan:
    def __init__(self, cols, taps, rows, owners):
        self.cols, self.taps, self.rows, self.owners = cols, taps, rows, owners
        self.granule = taps // 2
        self.held = cols // self.granule
        self.steps = [self.held * n // d for n, d in RATIOS]
        self.part_cols = [cols * n // d for n, d in RATIOS]
        self.part_rows = [rows * n // d for n, d in RATIOS]
        self.reach = max(2, 6 * owners // 16)
        self.most = max(sum(count for _, _, _, count, _ in self.sends(source)) for source in range(owners))

    def pieces(self, source, target):
        found = []
        for part, step in enumerate(self.steps):
            first = step * target - 1
            low = max(self.held * source, first)
            high = min(self.held * (source + 1), first + step + 2)
            if low < high and (part or source != target):
                found.append((part, target, low - self.held * source, high - low, low - first))
        return found

    def sends(self, source):
        near = range(max(0, source - 1), min(self.owners, 4 * source + 8))
        return [piece for target in near for piece in self.pieces(source, target)]

    def far(self, source, target):
        return target - source >= self.reach

    def targets(self, me, far):
        return [to for to in range(self.owners) if to != me and self.far(me, to) == far and self.pieces(me, to)]

    def sources(self, me, far):
        return [by for by in range(self.owners) if by != me and self.far(by, me) == far and self.pieces(by, me)]


def choose(me, low, high, act):
    if high - low == 1:
        act(low)
    else:
        middle = (low + high) // 2
        pl.when(me < middle)(lambda: choose(me, low, middle, act))
        pl.when(me >= middle)(lambda: choose(me, middle, high, act))


def one_hot(shape, make):
    left = lax.broadcasted_iota(jnp.int32, shape, 0)
    right = lax.broadcasted_iota(jnp.int32, shape, 1)
    return make(left, right).astype(jnp.float32).astype(jnp.bfloat16)


def build(window, shifts, low, high):
    width = (high - low + 1) * LANES
    start = low * LANES
    for which in (0, 1):
        line = window[which : which + 1, start : start + width].astype(jnp.float32)
        base = jnp.broadcast_to(line, (8, width))
        place = lax.broadcasted_iota(jnp.int32, (8, width), 0)
        for bit in (1, 2, 4):
            base = jnp.where((place & bit) != 0, pltpu.roll(base, width - bit, 1), base)
        base = jnp.concatenate([base, pltpu.roll(base, width - 8, 1)], 0).astype(jnp.bfloat16)
        for turn in range(LANES // TILE):
            moved = base if turn == 0 else pltpu.roll(base, width - TILE * turn, 1)
            for block in range(high - low):
                spot = (low + block) * LANES + TILE * turn
                shifts[which][spot : spot + TILE, :] = moved[:, block * LANES : (block + 1) * LANES]


def rows_of(lhs, count, which, tile):
    half, rows = lhs.shape[0] // 2, lhs.shape[1] // 2
    each = CHUNK // LANES
    slabs = [which * half + each * tile + at for at in range(each)]
    if count == rows:
        return jnp.concatenate([lhs[slab] for slab in slabs], 1)
    return jnp.concatenate(
        [jnp.concatenate([lhs[slab, :count], lhs[slab, rows : rows + count]], 0) for slab in slabs], 1
    )


def shifted(shifts, which, spot):
    start = CHUNK * spot
    return jnp.concatenate([shifts[which][start + at : start + at + CHUNK, :] for at in range(0, CHUNK, LANES)], 1)


def drive(queues):
    longest = max(len(queue) for queue in queues)
    for step in range(longest + 1):
        for unit, queue in enumerate(queues):
            if step < len(queue):
                pltpu.matmul_push_rhs(queue[step][0](), staging_register=step % 2, mxu_index=unit)
        for unit, queue in enumerate(queues):
            if 0 < step <= len(queue):
                for number, (acc, rows) in enumerate(queue[step - 1][1]):
                    pltpu.matmul_acc_lhs(acc, rows(), load_staged_rhs=None if number else (step - 1) % 2)


def taps_queue(lhs, shifts, count, accs, tiles, kinds, spots):
    return [
        (
            functools.partial(shifted, shifts, which, spot),
            [
                (acc, functools.partial(rows_of, lhs, count, which, spot - chunk))
                for chunk, acc in accs.items()
                if 0 <= spot - chunk < tiles
            ],
        )
        for spot in spots
        for which in kinds
    ]


def power(both):
    count = both.shape[0] // 2
    real, imag = both[:count], both[count:]
    return (real * real + imag * imag).astype(jnp.bfloat16)


def units(shapes):
    return [pltpu.ACC(unit)((rows, CHUNK), jnp.float32) for unit in (0, 1) for rows in shapes]


def planes_kernel(plan, spec_ref, index_ref, bank_ref, plane, plane3, win1, win2, lhs, win, win3, *refs):
    shifts, shifts3 = refs[:2], refs[2:4]
    bank, index, zeros, sized, in_sems, send_sem, recv_sems, ready = refs[4:]
    wins = (win, win1, win2, win3)
    rows, taps, size, cols, owners = plan.rows, plan.taps, plan.granule, plan.cols, plan.owners
    parts = len(RATIOS)
    me = lax.axis_index("freq")

    fetch_own = pltpu.make_async_copy(spec_ref, win.at[:, size : size + cols], in_sems.at[0])
    fetch_own.start()
    fetch_index = pltpu.make_async_copy(index_ref, index, in_sems.at[1])
    fetch_index.start()
    fetch_bank = pltpu.make_async_copy(bank_ref, bank, in_sems.at[2])
    fetch_bank.start()
    barrier = pltpu.get_barrier_semaphore()

    def signal(semaphore, peer):
        pl.semaphore_signal(semaphore, inc=1, device_id={"freq": peer}, device_id_type=pl.DeviceIdType.MESH)

    def greet(k):
        for peer in plan.sources(k, False) + plan.targets(k, True):
            signal(barrier, peer)

    choose(me, 0, owners, greet)
    zeros[...] = jnp.zeros(zeros.shape, zeros.dtype)

    def send(k, far):
        for part, to, begin, count, place in plan.sends(k):
            source = win.at[:, size * (1 + begin) : size * (1 + begin + count)]
            target = wins[part].at[:, size * place : size * (place + count)]
            if to == k:
                if not far:
                    pltpu.make_async_copy(source, target, recv_sems.at[part]).start()
            elif plan.far(k, to) == far:
                pltpu.make_async_remote_copy(
                    src_ref=source,
                    dst_ref=target,
                    send_sem=send_sem,
                    recv_sem=recv_sems.at[part],
                    device_id={"freq": to},
                    device_id_type=pl.DeviceIdType.MESH,
                ).start()

    def fill(part, spot):
        pltpu.make_async_copy(zeros, wins[part].at[:, spot : spot + size], recv_sems.at[part]).start()

    def first(k):
        count = len(plan.targets(k, False)) + len(plan.sources(k, True))
        if count:
            pl.semaphore_wait(barrier, count)
        send(k, False)
        for peer in plan.sources(k, True):
            signal(ready, peer)
        if k == 0:
            for part in range(parts):
                fill(part, 0)
        if k == owners - 1:
            fill(0, size + cols)

    def second(k):
        count = len(plan.targets(k, True))
        if count:
            pl.semaphore_wait(ready, count)
            send(k, True)

    def third(k):
        total = sum(count for _, to, _, count, _ in plan.sends(k) if to != k)
        if total:
            whole = sized.at[:, : total * size]
            pltpu.make_async_copy(whole, whole, send_sem).wait()

    def receive(part):
        whole = sized.at[:, : 2 * size if part == 0 else plan.part_cols[part] + taps]
        pltpu.make_async_copy(whole, whole, recv_sems.at[part]).wait()

    blocks = (cols + taps) // LANES - 1
    halo = size // LANES
    chunks = cols // CHUNK
    tiles = taps // CHUNK
    low, high = size // CHUNK, (size + cols) // CHUNK - 1

    fetch_own.wait()
    choose(me, 0, owners, first)
    build(win, shifts, halo, blocks - halo)
    fetch_index.wait()
    fetch_bank.wait()
    names = lax.broadcasted_iota(jnp.int32, (bank.shape[1], rows), 0)
    picks = (names == index[...]).astype(jnp.float32).T.astype(jnp.bfloat16)

    def gather(*accs):
        drive(
            [
                [
                    (
                        lambda deep=deep, wide=wide, unit=unit: bank[
                            unit, deep * CHUNK : (deep + 1) * CHUNK, wide * CHUNK : (wide + 1) * CHUNK
                        ],
                        [(accs[unit * tiles + wide], lambda deep=deep: picks[:, deep * CHUNK : (deep + 1) * CHUNK])],
                    )
                    for wide in range(tiles)
                    for deep in range(bank.shape[1] // CHUNK)
                ]
                for unit in (0, 1)
            ]
        )
        slabs = taps // LANES
        for tile in range(tiles):
            real = pltpu.matmul_pop(accs[tile]).astype(jnp.bfloat16)
            imag = pltpu.matmul_pop(accs[tiles + tile]).astype(jnp.bfloat16)
            for at in range(0, CHUNK, LANES):
                slab, piece = (tile * CHUNK + at) // LANES, slice(at, at + LANES)
                lhs[slab, :rows] = real[:, piece]
                lhs[slab, rows:] = imag[:, piece]
                lhs[slabs + slab, :rows] = -imag[:, piece]
                lhs[slabs + slab, rows:] = real[:, piece]

    pl.run_scoped(gather, *units([rows] * tiles))
    share = chunks // 2

    def part0(*accs):
        sides = [{share * unit + at: accs[share * unit + at] for at in range(share)} for unit in (0, 1)]

        def go(chosen):
            drive(
                [
                    taps_queue(lhs, shifts, rows, side, tiles, (0, 1), [spot for spot in order if chosen(spot)])
                    for side in sides
                    for order in [range(min(side), max(side) + tiles)]
                ]
            )

        def keep(chunk):
            plane[:, chunk * CHUNK : (chunk + 1) * CHUNK] = power(pltpu.matmul_pop(accs[chunk]))

        inner = [chunk for chunk in range(chunks) if low <= chunk and chunk + tiles <= high]
        go(lambda spot: low <= spot < high)
        for chunk in inner:
            keep(chunk)
        receive(0)
        build(win, shifts, 0, halo)
        build(win, shifts, blocks - halo, blocks)
        go(lambda spot: not low <= spot < high)
        for chunk in range(chunks):
            if chunk not in inner:
                keep(chunk)

    pl.run_scoped(part0, *units([2 * rows] * share))
    receive(3)
    build(win3, shifts3, 0, (plan.part_cols[3] + taps) // LANES - 1)
    count3 = plan.part_rows[3]
    share3 = plan.part_cols[3] // CHUNK // 2

    def part3(*accs):
        sides = [{share3 * unit + at: accs[share3 * unit + at] for at in range(share3)} for unit in (0, 1)]
        drive(
            [
                taps_queue(lhs, shifts3, count3, side, tiles, (0, 1), range(min(side), max(side) + tiles))
                for side in sides
            ]
        )
        for chunk, acc in enumerate(accs):
            plane3[:, chunk * CHUNK : (chunk + 1) * CHUNK] = power(pltpu.matmul_pop(acc))

    pl.run_scoped(part3, *units([2 * count3] * share3))
    choose(me, 0, owners, second)
    choose(me, 0, owners, third)
    receive(1)
    receive(2)


def sum_kernel(plan, plane, plane3, win1, win2, lhs, out_ref, out, plane1, plane2, *refs):
    shifts1, shifts2, cells, sems = refs[:2], refs[2:4], refs[4], refs[5]
    planes = (plane, plane1, plane2, plane3)
    parts = len(RATIOS)
    chunks, taps = plan.cols // CHUNK, plan.taps
    tiles = taps // CHUNK
    belows = [sum(plan.part_rows[1:part]) for part in range(parts)]

    def put(chunk):
        spot = slice(chunk * CHUNK, (chunk + 1) * CHUNK)
        return pltpu.make_async_copy(out.at[:, spot], out_ref.at[:, spot], sems.at[chunk])

    def make(part, shifts, window):
        build(window, shifts, 0, (plan.part_cols[part] + taps) // LANES - 1)

    def fill(part, shifts):
        count, number = plan.part_rows[part], plan.part_cols[part] // CHUNK

        def go(*accs):
            sides = [dict(enumerate(accs[unit * number : (unit + 1) * number])) for unit in (0, 1)]
            drive(
                [
                    taps_queue(lhs, shifts, count, side, tiles, (unit,), range(number + tiles - 1))
                    for unit, side in enumerate(sides)
                ]
            )
            for chunk in range(number):
                both = pltpu.matmul_pop(sides[0][chunk]) + pltpu.matmul_pop(sides[1][chunk])
                planes[part][:, chunk * CHUNK : (chunk + 1) * CHUNK] = power(both)

        pl.run_scoped(go, *units([2 * count] * number))

    def place(part, chunk):
        start = CHUNK * RATIOS[part][0] // RATIOS[part][1] * chunk
        base = min(start // LANES * LANES, plan.part_cols[part] - CHUNK)
        return base, start - base

    def stretch(part):
        n, d = RATIOS[part]
        count, below = plan.part_rows[part], belows[part]

        def go(*accs):
            queues, drained = [], []
            for unit in (0, 1):
                mine = list(range(unit, chunks, 2))
                refs_of = dict(zip(mine, accs[unit * len(mine) : (unit + 1) * len(mine)]))
                skips = sorted({place(part, chunk)[1] for chunk in mine})
                queues.append(
                    [
                        (
                            lambda skip=skip: one_hot((CHUNK, CHUNK), lambda k, r: k == skip + r * n // d),
                            [
                                (
                                    refs_of[chunk],
                                    lambda base=place(part, chunk)[0]: planes[part][:, base : base + CHUNK],
                                )
                                for chunk in mine
                                if place(part, chunk)[1] == skip
                            ],
                        )
                        for skip in skips
                    ]
                )
                drained += list(refs_of.items())
            drive(queues)
            for chunk, acc in sorted(drained, key=lambda item: item[0]):
                cells[chunk, below : below + count] = pltpu.matmul_pop(acc).astype(jnp.bfloat16)

        pl.run_scoped(go, *units([count] * (chunks // 2)))

    left = lax.broadcasted_iota(jnp.int32, (plan.rows, CHUNK), 0)
    right = lax.broadcasted_iota(jnp.int32, (plan.rows, CHUNK), 1)
    pick = None
    for part in range(1, parts):
        n, d = RATIOS[part]
        hit = right == belows[part] + left * n // d
        pick = hit if pick is None else pick | hit
    pick = pick.astype(jnp.float32).astype(jnp.bfloat16)

    used = sum(plan.part_rows[1:])
    for chunk in range(chunks):
        cells[chunk, used:] = jnp.zeros((CHUNK - used, CHUNK), cells.dtype)
    make(2, shifts2, win2)
    stretch(3)
    fill(2, shifts2)
    make(1, shifts1, win1)
    stretch(2)
    fill(1, shifts1)
    stretch(1)

    def total(*accs):
        drive([[(lambda chunk=chunk: cells[chunk], [(accs[chunk // 2 + unit * (chunks // 2)], lambda: pick)])
                for chunk in range(unit, chunks, 2)] for unit in (0, 1)])
        for chunk in range(chunks):
            spot = slice(chunk * CHUNK, (chunk + 1) * CHUNK)
            acc = accs[chunk // 2 + chunk % 2 * (chunks // 2)]
            out[:, spot] = plane[:, spot].astype(jnp.float32) + pltpu.matmul_pop(acc)
            put(chunk).start()

    pl.run_scoped(total, *units([plan.rows] * (chunks // 2)))
    for chunk in range(chunks):
        put(chunk).wait()


def body(spectrum, template_bank, template_index):
    owners = lax.axis_size("freq")
    taps = template_bank.shape[2]
    rows = template_index.shape[0]
    cols = spectrum.shape[1]
    plan = Plan(cols, taps, rows, owners)
    hbm = pl.BlockSpec(memory_space=pltpu.HBM)
    vmem = pl.BlockSpec(memory_space=pltpu.VMEM)
    wide = [width + taps for width in plan.part_cols]

    def held(*shape, kind=jnp.bfloat16):
        return pltpu.VMEM(shape, kind)

    between = (
        held(rows, cols),
        held(plan.part_rows[3], plan.part_cols[3]),
        held(2, wide[1]),
        held(2, wide[2]),
        held(2 * taps // LANES, 2 * rows, LANES),
    )
    inputs = (spectrum, template_index.reshape(1, rows), template_bank)
    results = pl.pallas_call(
        functools.partial(planes_kernel, plan),
        out_shape=between,
        in_specs=[hbm] * 3,
        out_specs=(vmem,) * len(between),
        scratch_shapes=[
            held(2, wide[0]),
            held(2, wide[3]),
            *[held(wide[part], LANES) for part in (0, 0, 3, 3)],
            held(*template_bank.shape),
            held(1, rows, kind=jnp.int32),
            held(2, plan.granule),
            held(2, max(plan.granule * plan.most, *wide)),
            pltpu.SemaphoreType.DMA((3,)),
            pltpu.SemaphoreType.DMA,
            pltpu.SemaphoreType.DMA((len(RATIOS),)),
            pltpu.SemaphoreType.REGULAR,
        ],
        compiler_params=pltpu.CompilerParams(collective_id=0, has_side_effects=True, vmem_limit_bytes=24 * 2**20),
        name="planes",
    )(*[pltpu.with_memory_space_constraint(x, pltpu.HBM) for x in inputs])
    return pl.pallas_call(
        functools.partial(sum_kernel, plan),
        out_shape=jax.ShapeDtypeStruct((rows, cols), jnp.float32),
        in_specs=[vmem] * len(between),
        out_specs=hbm,
        scratch_shapes=[
            held(rows, cols, kind=jnp.float32),
            *[held(plan.part_rows[part], plan.part_cols[part]) for part in (1, 2)],
            *[held(wide[part], LANES) for part in (1, 1, 2, 2)],
            held(cols // CHUNK, CHUNK, CHUNK),
            pltpu.SemaphoreType.DMA((cols // CHUNK,)),
        ],
        compiler_params=pltpu.CompilerParams(vmem_limit_bytes=24 * 2**20),
        name="sums",
    )(*results)


def solution(mesh):
    return jax.shard_map(
        body,
        mesh=mesh,
        in_specs=(P(None, ("beam", "freq")), P(), P()),
        out_specs=P(None, ("beam", "freq")),
        check_vma=False,
    )
```

```python
import functools

import jax
import jax.numpy as jnp
from jax import lax
from jax.experimental import pallas as pl
from jax.experimental.pallas import tpu as pltpu
from jax.sharding import PartitionSpec as P

RATIOS = ((1, 1), (1, 2), (1, 4), (3, 4))
CHUNK = 256
LANES = 128
TILE = 16


class Plan:
    def __init__(self, cols, taps, rows, owners):
        self.cols, self.taps, self.rows, self.owners = cols, taps, rows, owners
        self.granule = taps // 2
        self.held = cols // self.granule
        self.steps = [self.held * n // d for n, d in RATIOS]
        self.part_cols = [cols * n // d for n, d in RATIOS]
        self.part_rows = [rows * n // d for n, d in RATIOS]
        self.reach = max(2, 6 * owners // 16)
        self.most = max(sum(count for _, _, _, count, _ in self.sends(source)) for source in range(owners))

    def pieces(self, source, target):
        found = []
        for part, step in enumerate(self.steps):
            first = step * target - 1
            low = max(self.held * source, first)
            high = min(self.held * (source + 1), first + step + 2)
            if low < high and (part or source != target):
                found.append((part, target, low - self.held * source, high - low, low - first))
        return found

    def sends(self, source):
        near = range(max(0, source - 1), min(self.owners, 4 * source + 8))
        return [piece for target in near for piece in self.pieces(source, target)]

    def far(self, source, target):
        return target - source >= self.reach

    def targets(self, me, far):
        return [to for to in range(self.owners) if to != me and self.far(me, to) == far and self.pieces(me, to)]

    def sources(self, me, far):
        return [by for by in range(self.owners) if by != me and self.far(by, me) == far and self.pieces(by, me)]


def choose(me, low, high, act):
    if high - low == 1:
        act(low)
    else:
        middle = (low + high) // 2
        pl.when(me < middle)(lambda: choose(me, low, middle, act))
        pl.when(me >= middle)(lambda: choose(me, middle, high, act))


def one_hot(shape, make):
    left = lax.broadcasted_iota(jnp.int32, shape, 0)
    right = lax.broadcasted_iota(jnp.int32, shape, 1)
    return make(left, right).astype(jnp.float32).astype(jnp.bfloat16)


def build(window, shifts, low, high):
    width = (high - low + 1) * LANES
    start = low * LANES
    bases = []

    def first(which):
        line = window[which : which + 1, start : start + width].astype(jnp.float32)
        base = jnp.broadcast_to(line, (8, width))
        place = lax.broadcasted_iota(jnp.int32, (8, width), 0)
        for bit in (1, 2, 4):
            base = jnp.where((place & bit) != 0, pltpu.roll(base, width - bit, 1), base)
        bases.append(jnp.concatenate([base, pltpu.roll(base, width - 8, 1)], 0).astype(jnp.bfloat16))

    def turned(which, turn):
        base = bases[which]
        moved = base if turn == 0 else pltpu.roll(base, width - TILE * turn, 1)
        for block in range(high - low):
            spot = (low + block) * LANES + TILE * turn
            shifts[which][spot : spot + TILE, :] = moved[:, block * LANES : (block + 1) * LANES]

    tasks = [functools.partial(first, which) for which in (0, 1)]
    return tasks + [functools.partial(turned, which, turn) for turn in range(LANES // TILE) for which in (0, 1)]


def run(tasks):
    for task in tasks:
        task()


def rows_of(lhs, count, which, tile):
    half, rows = lhs.shape[0] // 2, lhs.shape[1] // 2
    each = CHUNK // LANES
    slabs = [which * half + each * tile + at for at in range(each)]
    if count == rows:
        return jnp.concatenate([lhs[slab] for slab in slabs], 1)
    return jnp.concatenate(
        [jnp.concatenate([lhs[slab, :count], lhs[slab, rows : rows + count]], 0) for slab in slabs], 1
    )


def shifted(shifts, which, spot):
    start = CHUNK * spot
    return jnp.concatenate([shifts[which][start + at : start + at + CHUNK, :] for at in range(0, CHUNK, LANES)], 1)


def drive(queues, tasks=()):
    longest = max(len(queue) for queue in queues)
    done = 0
    for step in range(longest + 1):
        for unit, queue in enumerate(queues):
            if step < len(queue):
                pltpu.matmul_push_rhs(queue[step][0](), staging_register=step % 2, mxu_index=unit)
        for unit, queue in enumerate(queues):
            if 0 < step <= len(queue):
                for number, (acc, rows) in enumerate(queue[step - 1][1]):
                    pltpu.matmul_acc_lhs(acc, rows(), load_staged_rhs=None if number else (step - 1) % 2)
        until = len(tasks) * (step + 1) // (longest + 1)
        run(tasks[done:until])
        done = until


def taps_queue(lhs, shifts, count, accs, tiles, kinds, spots):
    return [
        (
            functools.partial(shifted, shifts, which, spot),
            [
                (acc, functools.partial(rows_of, lhs, count, which, spot - chunk))
                for chunk, acc in accs.items()
                if 0 <= spot - chunk < tiles
            ],
        )
        for spot in spots
        for which in kinds
    ]


def power(both):
    count = both.shape[0] // 2
    real, imag = both[:count], both[count:]
    return (real * real + imag * imag).astype(jnp.bfloat16)


def units(shapes):
    return [pltpu.ACC(unit)((rows, CHUNK), jnp.float32) for unit in (0, 1) for rows in shapes]


class Spread:
    def __init__(self, plan):
        self.plan = plan
        self.chunks = plan.cols // CHUNK
        self.belows = [sum(plan.part_rows[1:part]) for part in range(len(RATIOS))]
        self.used = sum(plan.part_rows[1:])
        self.tables = sorted(
            {(part, self.place(part, chunk)[1]) for part in range(1, len(RATIOS)) for chunk in range(self.chunks)}
        )

    def place(self, part, chunk):
        start = CHUNK * RATIOS[part][0] // RATIOS[part][1] * chunk
        base = min(start // LANES * LANES, self.plan.part_cols[part] - CHUNK)
        return base, start - base

    def prepare(self, tables, pick, cells):
        for number, (part, skip) in enumerate(self.tables):
            n, d = RATIOS[part]
            tables[number] = one_hot((CHUNK, CHUNK), lambda k, r: k == skip + r * n // d)
        left = lax.broadcasted_iota(jnp.int32, pick.shape, 0)
        right = lax.broadcasted_iota(jnp.int32, pick.shape, 1)
        hits = [right == self.belows[part] + left * n // d for part, (n, d) in enumerate(RATIOS) if part]
        pick[...] = functools.reduce(jnp.logical_or, hits).astype(jnp.float32).astype(jnp.bfloat16)
        for chunk in range(self.chunks):
            cells[chunk, self.used :] = jnp.zeros((CHUNK - self.used, CHUNK), cells.dtype)

    def queues(self, part, plane, tables, accs):
        half = self.chunks // 2
        found = []
        for unit in (0, 1):
            mine = list(range(unit, self.chunks, 2))
            queue = []
            for skip in sorted({self.place(part, chunk)[1] for chunk in mine}):
                number = self.tables.index((part, skip))
                users = []
                for chunk in mine:
                    base, skipped = self.place(part, chunk)
                    if skipped == skip:
                        users.append((accs[unit * half + chunk // 2], lambda base=base: plane[:, base : base + CHUNK]))
                queue.append((lambda number=number: tables[number], users))
            found.append(queue)
        return found

    def drain(self, part, accs, cells):
        count, below = self.plan.part_rows[part], self.belows[part]
        for chunk in range(self.chunks):
            acc = accs[chunk % 2 * (self.chunks // 2) + chunk // 2]
            cells[chunk, below : below + count] = pltpu.matmul_pop(acc).astype(jnp.bfloat16)


def planes_kernel(plan, spec_ref, index_ref, bank_ref, plane, cells, tables, pick, win1, win2, lhs, win, win3, *refs):
    shifts, shifts3 = refs[:2], refs[2:4]
    plane3, bank, index, zeros, sized, in_sems, send_sem, recv_sems, ready = refs[4:]
    wins = (win, win1, win2, win3)
    rows, taps, size, cols, owners = plan.rows, plan.taps, plan.granule, plan.cols, plan.owners
    parts = len(RATIOS)
    me = lax.axis_index("freq")

    fetch_own = pltpu.make_async_copy(spec_ref, win.at[:, size : size + cols], in_sems.at[0])
    fetch_own.start()
    fetch_index = pltpu.make_async_copy(index_ref, index, in_sems.at[1])
    fetch_index.start()
    fetch_bank = [
        pltpu.make_async_copy(bank_ref.at[:, :, slab * LANES : (slab + 1) * LANES], bank.at[slab], in_sems.at[2 + slab])
        for slab in range(taps // LANES)
    ]
    run([fetch.start for fetch in fetch_bank])
    barrier = pltpu.get_barrier_semaphore()

    def signal(semaphore, peer):
        pl.semaphore_signal(semaphore, inc=1, device_id={"freq": peer}, device_id_type=pl.DeviceIdType.MESH)

    def greet(k):
        for peer in plan.sources(k, False) + plan.targets(k, True):
            signal(barrier, peer)

    choose(me, 0, owners, greet)
    zeros[...] = jnp.zeros(zeros.shape, zeros.dtype)

    def send(k, far):
        for part, to, begin, count, place in plan.sends(k):
            source = win.at[:, size * (1 + begin) : size * (1 + begin + count)]
            target = wins[part].at[:, size * place : size * (place + count)]
            if to == k:
                if not far:
                    pltpu.make_async_copy(source, target, recv_sems.at[part]).start()
            elif plan.far(k, to) == far:
                pltpu.make_async_remote_copy(
                    src_ref=source,
                    dst_ref=target,
                    send_sem=send_sem,
                    recv_sem=recv_sems.at[part],
                    device_id={"freq": to},
                    device_id_type=pl.DeviceIdType.MESH,
                ).start()

    def fill(part, spot):
        pltpu.make_async_copy(zeros, wins[part].at[:, spot : spot + size], recv_sems.at[part]).start()

    def first(k):
        count = len(plan.targets(k, False)) + len(plan.sources(k, True))
        if count:
            pl.semaphore_wait(barrier, count)
        send(k, False)
        for peer in plan.sources(k, True):
            signal(ready, peer)
        if k == 0:
            for part in range(parts):
                fill(part, 0)
        if k == owners - 1:
            fill(0, size + cols)

    def second(k):
        count = len(plan.targets(k, True))
        if count:
            pl.semaphore_wait(ready, count)
            send(k, True)

    def third(k):
        total = sum(count for _, to, _, count, _ in plan.sends(k) if to != k)
        if total:
            whole = sized.at[:, : total * size]
            pltpu.make_async_copy(whole, whole, send_sem).wait()

    def receive(part):
        whole = sized.at[:, : 2 * size if part == 0 else plan.part_cols[part] + taps]
        pltpu.make_async_copy(whole, whole, recv_sems.at[part]).wait()

    blocks = (cols + taps) // LANES - 1
    halo = size // LANES
    chunks = cols // CHUNK
    tiles = taps // CHUNK
    low, high = size // CHUNK, (size + cols) // CHUNK - 1

    spread = Spread(plan)
    spread.prepare(tables, pick, cells)
    fetch_own.wait()
    choose(me, 0, owners, first)
    fetch_index.wait()
    run([fetch.wait for fetch in fetch_bank])
    names = lax.broadcasted_iota(jnp.int32, (bank.shape[2], rows), 0)
    picks = (names == index[...]).astype(jnp.float32).T.astype(jnp.bfloat16)

    def gather(*accs):
        drive(
            [
                [
                    (
                        lambda deep=deep, wide=wide, unit=unit: jnp.concatenate(
                            [
                                bank[wide * CHUNK // LANES + at, unit, deep * CHUNK : (deep + 1) * CHUNK]
                                for at in range(CHUNK // LANES)
                            ],
                            1,
                        ),
                        [(accs[unit * tiles + wide], lambda deep=deep: picks[:, deep * CHUNK : (deep + 1) * CHUNK])],
                    )
                    for wide in range(tiles)
                    for deep in range(bank.shape[2] // CHUNK)
                ]
                for unit in (0, 1)
            ],
            build(win, shifts, halo, blocks - halo),
        )
        slabs = taps // LANES
        for tile in range(tiles):
            real = pltpu.matmul_pop(accs[tile]).astype(jnp.bfloat16)
            imag = pltpu.matmul_pop(accs[tiles + tile]).astype(jnp.bfloat16)
            for at in range(0, CHUNK, LANES):
                slab, piece = (tile * CHUNK + at) // LANES, slice(at, at + LANES)
                lhs[slab, :rows] = real[:, piece]
                lhs[slab, rows:] = imag[:, piece]
                lhs[slabs + slab, :rows] = -imag[:, piece]
                lhs[slabs + slab, rows:] = real[:, piece]

    pl.run_scoped(gather, *units([rows] * tiles))
    share = chunks // 2

    def part0(*accs):
        sides = [{share * unit + at: accs[share * unit + at] for at in range(share)} for unit in (0, 1)]

        def go(chosen, tasks=()):
            drive(
                [
                    taps_queue(lhs, shifts, rows, side, tiles, (0, 1), [spot for spot in order if chosen(spot)])
                    for side in sides
                    for order in [range(min(side), max(side) + tiles)]
                ],
                tasks,
            )

        def keep(chunk):
            plane[:, chunk * CHUNK : (chunk + 1) * CHUNK] = power(pltpu.matmul_pop(accs[chunk]))

        inner = [chunk for chunk in range(chunks) if low <= chunk and chunk + tiles <= high]
        go(lambda spot: low <= spot < high)
        for chunk in inner:
            keep(chunk)
        receive(0)
        receive(3)
        run(build(win, shifts, 0, halo) + build(win, shifts, blocks - halo, blocks))
        go(lambda spot: not low <= spot < high, build(win3, shifts3, 0, (plan.part_cols[3] + taps) // LANES - 1))
        for chunk in range(chunks):
            if chunk not in inner:
                keep(chunk)

    pl.run_scoped(part0, *units([2 * rows] * share))
    choose(me, 0, owners, second)
    count3 = plan.part_rows[3]
    share3 = plan.part_cols[3] // CHUNK // 2

    def part3(*accs):
        sides = [{share3 * unit + at: accs[share3 * unit + at] for at in range(share3)} for unit in (0, 1)]
        drive(
            [
                taps_queue(lhs, shifts3, count3, side, tiles, (0, 1), range(min(side), max(side) + tiles))
                for side in sides
            ]
        )
        for chunk, acc in enumerate(accs):
            plane3[:, chunk * CHUNK : (chunk + 1) * CHUNK] = power(pltpu.matmul_pop(acc))

    pl.run_scoped(part3, *units([2 * count3] * share3))

    def spread3(*accs):
        drive(spread.queues(3, plane3, tables, accs))
        spread.drain(3, accs, cells)

    pl.run_scoped(spread3, *units([count3] * (chunks // 2)))
    choose(me, 0, owners, third)
    receive(1)
    receive(2)


def sum_kernel(plan, plane, before, tables, pick, win1, win2, lhs, out_ref, out, cells, plane1, plane2, *refs):
    shifts1, shifts2, sems = refs[:2], refs[2:4], refs[4]
    chunks, taps = plan.cols // CHUNK, plan.taps
    tiles = taps // CHUNK
    spread = Spread(plan)
    below = spread.belows[3]
    count1, count2 = plan.part_rows[1], plan.part_rows[2]
    number1, number2 = plan.part_cols[1] // CHUNK, plan.part_cols[2] // CHUNK

    def put(chunk):
        spot = slice(chunk * CHUNK, (chunk + 1) * CHUNK)
        return pltpu.make_async_copy(out.at[:, spot], out_ref.at[:, spot], sems.at[chunk])

    def make(part, shifts, window):
        return build(window, shifts, 0, (plan.part_cols[part] + taps) // LANES - 1)

    def fill(count, shifts, sides):
        number = len(sides[0])
        return [
            taps_queue(lhs, shifts, count, dict(enumerate(side)), tiles, (unit,), range(number + tiles - 1))
            for unit, side in enumerate(sides)
        ]

    def keep(into, sides):
        for chunk, (left, right) in enumerate(zip(*sides)):
            both = pltpu.matmul_pop(left) + pltpu.matmul_pop(right)
            into[:, chunk * CHUNK : (chunk + 1) * CHUNK] = power(both)

    def parts(*accs):
        each = len(accs) // 2
        sides = [accs[:each], accs[each:]]
        sides2 = [side[:number2] for side in sides]
        sides1 = [side[number2 : number2 + number1] for side in sides]
        spreads = [acc for side in sides for acc in side[number2 + number1 :]]
        run(make(2, shifts2, win2))
        drive(fill(count2, shifts2, sides2), make(1, shifts1, win1))
        keep(plane2, sides2)
        stretches = spread.queues(2, plane2, tables, spreads)
        drive([queue + stretch for queue, stretch in zip(fill(count1, shifts1, sides1), stretches)])
        keep(plane1, sides1)
        spread.drain(2, spreads, cells)

    pl.run_scoped(parts, *units([2 * count2] * number2 + [2 * count1] * number1 + [count2] * (chunks // 2)))
    for chunk in range(chunks):
        cells[chunk, below:] = before[chunk, below:]

    def total(*accs):
        each = len(accs) // 2
        half = chunks // 2
        spreads = [acc for unit in (0, 1) for acc in accs[unit * each : unit * each + half]]
        totals = [accs[chunk % 2 * each + half + chunk // 2] for chunk in range(chunks)]
        drive(spread.queues(1, plane1, tables, spreads))
        spread.drain(1, spreads, cells)
        drive(
            [
                [
                    (lambda chunk=chunk: cells[chunk], [(totals[chunk], lambda: pick[...])])
                    for chunk in range(unit, chunks, 2)
                ]
                for unit in (0, 1)
            ]
        )
        for chunk in range(chunks):
            spot = slice(chunk * CHUNK, (chunk + 1) * CHUNK)
            out[:, spot] = plane[:, spot].astype(jnp.float32) + pltpu.matmul_pop(totals[chunk])
            put(chunk).start()

    pl.run_scoped(total, *units([count1] * (chunks // 2) + [plan.rows] * (chunks // 2)))
    for chunk in range(chunks):
        put(chunk).wait()


def body(spectrum, template_bank, template_index):
    owners = lax.axis_size("freq")
    taps = template_bank.shape[2]
    rows = template_index.shape[0]
    cols = spectrum.shape[1]
    plan = Plan(cols, taps, rows, owners)
    hbm = pl.BlockSpec(memory_space=pltpu.HBM)
    vmem = pl.BlockSpec(memory_space=pltpu.VMEM)
    wide = [width + taps for width in plan.part_cols]

    def held(*shape, kind=jnp.bfloat16):
        return pltpu.VMEM(shape, kind)

    between = (
        held(rows, cols),
        held(cols // CHUNK, CHUNK, CHUNK),
        held(len(Spread(plan).tables), CHUNK, CHUNK),
        held(rows, CHUNK),
        held(2, wide[1]),
        held(2, wide[2]),
        held(2 * taps // LANES, 2 * rows, LANES),
    )
    inputs = (spectrum, template_index.reshape(1, rows), template_bank)
    results = pl.pallas_call(
        functools.partial(planes_kernel, plan),
        out_shape=between,
        in_specs=[hbm] * 3,
        out_specs=(vmem,) * len(between),
        scratch_shapes=[
            held(2, wide[0]),
            held(2, wide[3]),
            *[held(wide[part], LANES) for part in (0, 0, 3, 3)],
            held(plan.part_rows[3], plan.part_cols[3]),
            held(taps // LANES, *template_bank.shape[:2], LANES),
            held(1, rows, kind=jnp.int32),
            held(2, plan.granule),
            held(2, max(plan.granule * plan.most, *wide)),
            pltpu.SemaphoreType.DMA((2 + taps // LANES,)),
            pltpu.SemaphoreType.DMA,
            pltpu.SemaphoreType.DMA((len(RATIOS),)),
            pltpu.SemaphoreType.REGULAR,
        ],
        compiler_params=pltpu.CompilerParams(collective_id=0, has_side_effects=True, vmem_limit_bytes=24 * 2**20),
        name="planes",
    )(*[pltpu.with_memory_space_constraint(x, pltpu.HBM) for x in inputs])
    return pl.pallas_call(
        functools.partial(sum_kernel, plan),
        out_shape=jax.ShapeDtypeStruct((rows, cols), jnp.float32),
        in_specs=[vmem] * len(between),
        out_specs=hbm,
        scratch_shapes=[
            held(rows, cols, kind=jnp.float32),
            held(cols // CHUNK, CHUNK, CHUNK),
            *[held(plan.part_rows[part], plan.part_cols[part]) for part in (1, 2)],
            *[held(wide[part], LANES) for part in (1, 1, 2, 2)],
            pltpu.SemaphoreType.DMA((cols // CHUNK,)),
        ],
        compiler_params=pltpu.CompilerParams(vmem_limit_bytes=24 * 2**20),
        name="sums",
    )(*results)


def solution(mesh):
    return jax.shard_map(
        body,
        mesh=mesh,
        in_specs=(P(None, ("beam", "freq")), P(), P()),
        out_specs=P(None, ("beam", "freq")),
        check_vma=False,
    )
```

```python
import functools

import jax
import jax.numpy as jnp
from jax import lax
from jax.experimental import pallas as pl
from jax.experimental.pallas import tpu as pltpu
from jax.sharding import PartitionSpec as P

RATIOS = ((1, 1), (1, 2), (1, 4), (3, 4))
CHUNK = 256
LANES = 128
TILE = 16


class Plan:
    def __init__(self, cols, taps, rows, owners):
        self.cols, self.taps, self.rows, self.owners = cols, taps, rows, owners
        self.granule = taps // 2
        self.held = cols // self.granule
        self.steps = [self.held * n // d for n, d in RATIOS]
        self.part_cols = [cols * n // d for n, d in RATIOS]
        self.part_rows = [rows * n // d for n, d in RATIOS]
        self.reach = max(2, 6 * owners // 16)
        self.most = max(sum(count for _, _, _, count, _ in self.sends(source)) for source in range(owners))

    def pieces(self, source, target):
        found = []
        for part, step in enumerate(self.steps):
            first = step * target - 1
            low = max(self.held * source, first)
            high = min(self.held * (source + 1), first + step + 2)
            if low < high and (part or source != target):
                found.append((part, target, low - self.held * source, high - low, low - first))
        return found

    def sends(self, source):
        near = range(max(0, source - 1), min(self.owners, 4 * source + 8))
        return [piece for target in near for piece in self.pieces(source, target)]

    def far(self, source, target):
        return target - source >= self.reach

    def targets(self, me, far):
        return [to for to in range(self.owners) if to != me and self.far(me, to) == far and self.pieces(me, to)]

    def sources(self, me, far):
        return [by for by in range(self.owners) if by != me and self.far(by, me) == far and self.pieces(by, me)]


def choose(me, low, high, act):
    if high - low == 1:
        act(low)
    else:
        middle = (low + high) // 2
        pl.when(me < middle)(lambda: choose(me, low, middle, act))
        pl.when(me >= middle)(lambda: choose(me, middle, high, act))


def one_hot(shape, make):
    left = lax.broadcasted_iota(jnp.int32, shape, 0)
    right = lax.broadcasted_iota(jnp.int32, shape, 1)
    return make(left, right).astype(jnp.float32).astype(jnp.bfloat16)


def fill_bases(window, bases, low, high, spare=0):
    width = (high - low) * LANES
    for which in (0, 1):
        line = window[which : which + 1, low * LANES : high * LANES].astype(jnp.float32)
        base = jnp.broadcast_to(line, (8, width))
        place = lax.broadcasted_iota(jnp.int32, (8, width), 0)
        for bit in (1, 2, 4):
            base = jnp.where((place & bit) != 0, pltpu.roll(base, width - bit, 1), base)
        base = jnp.concatenate([base, pltpu.roll(base, width - 8, 1)], 0).astype(jnp.bfloat16)
        for block in range(low, high - spare):
            bases[which, block] = base[:, (block - low) * LANES : (block - low + 1) * LANES]


class Shifts:
    def __init__(self, bases):
        self.bases = bases
        self.turned, self.blocks = {}, {}
        lane = lax.broadcasted_iota(jnp.int32, (TILE, LANES), 1)
        self.keep = [lane < LANES - TILE * turn for turn in range(LANES // TILE)]

    def turn(self, which, block, turn):
        key = which, block, turn
        if key not in self.turned:
            value = self.bases[which, block]
            self.turned[key] = pltpu.roll(value, LANES - TILE * turn, 1) if turn else value
        return self.turned[key]

    def block(self, which, block):
        key = which, block
        if key not in self.blocks:
            rows = [self.turn(which, block, 0)]
            for turn in range(1, LANES // TILE):
                rows.append(
                    jnp.where(self.keep[turn], self.turn(which, block, turn), self.turn(which, block + 1, turn))
                )
            self.blocks[key] = jnp.concatenate(rows, 0)
        return self.blocks[key]

    def tile(self, which, spot):
        each = CHUNK // LANES
        return jnp.concatenate(
            [
                jnp.concatenate([self.block(which, each * spot + at + row) for row in range(each)], 0)
                for at in range(each)
            ],
            1,
        )


def run(tasks):
    for task in tasks:
        task()


def rows_of(lhs, first, count, which, tile):
    half = lhs.shape[0] // 2
    each = CHUNK // LANES
    slabs = [which * half + each * tile + at for at in range(each)]
    return jnp.concatenate(
        [jnp.concatenate([lhs[slab, row : row + count] for row in first], 0) for slab in slabs], 1
    )


def drive(queues):
    longest = max(len(queue) for queue in queues)
    for step in range(longest + 1):
        for unit, queue in enumerate(queues):
            if step < len(queue):
                pltpu.matmul_push_rhs(queue[step][0](), staging_register=step % 2, mxu_index=unit)
        for unit, queue in enumerate(queues):
            if 0 < step <= len(queue):
                for number, (acc, rows) in enumerate(queue[step - 1][1]):
                    pltpu.matmul_acc_lhs(acc, rows(), load_staged_rhs=None if number else (step - 1) % 2)


def taps_queue(lhs, shifts, first, count, accs, tiles, kinds, spots):
    return [
        (
            functools.partial(shifts.tile, which, spot),
            [
                (acc, functools.partial(rows_of, lhs, first, count, which, spot - chunk))
                for chunk, acc in accs.items()
                if 0 <= spot - chunk < tiles
            ],
        )
        for which in kinds
        for spot in spots
    ]


def power(real, imag):
    return (real * real + imag * imag).astype(jnp.bfloat16)


def units(shapes):
    return [pltpu.ACC(unit)((rows, CHUNK), jnp.float32) for unit in (0, 1) for rows in shapes]


class Spread:
    def __init__(self, plan):
        self.plan = plan
        self.chunks = plan.cols // CHUNK
        self.belows = [sum(plan.part_rows[1:part]) for part in range(len(RATIOS))]
        self.used = sum(plan.part_rows[1:])
        self.tables = sorted(
            {(part, self.place(part, chunk)[1]) for part in range(1, len(RATIOS)) for chunk in range(self.chunks)}
        )

    def place(self, part, chunk):
        start = CHUNK * RATIOS[part][0] // RATIOS[part][1] * chunk
        base = min(start // LANES * LANES, self.plan.part_cols[part] - CHUNK)
        return base, start - base

    def prepare(self, tables, pick, cells):
        for number, (part, skip) in enumerate(self.tables):
            n, d = RATIOS[part]
            tables[number] = one_hot((CHUNK, CHUNK), lambda k, r: k == skip + r * n // d)
        left = lax.broadcasted_iota(jnp.int32, pick.shape, 0)
        right = lax.broadcasted_iota(jnp.int32, pick.shape, 1)
        hits = [right == self.belows[part] + left * n // d for part, (n, d) in enumerate(RATIOS) if part]
        pick[...] = functools.reduce(jnp.logical_or, hits).astype(jnp.float32).astype(jnp.bfloat16)
        for chunk in range(self.chunks):
            cells[chunk, self.used :] = jnp.zeros((CHUNK - self.used, CHUNK), cells.dtype)

    def queues(self, part, plane, tables, accs):
        half = self.chunks // 2
        found = []
        for unit in (0, 1):
            mine = list(range(unit, self.chunks, 2))
            queue = []
            for skip in sorted({self.place(part, chunk)[1] for chunk in mine}):
                number = self.tables.index((part, skip))
                users = []
                for chunk in mine:
                    base, skipped = self.place(part, chunk)
                    if skipped == skip:
                        users.append((accs[unit * half + chunk // 2], lambda base=base: plane[:, base : base + CHUNK]))
                queue.append((lambda number=number: tables[number], users))
            found.append(queue)
        return found

    def drain(self, part, accs, cells):
        count, below = self.plan.part_rows[part], self.belows[part]
        for chunk in range(self.chunks):
            acc = accs[chunk % 2 * (self.chunks // 2) + chunk // 2]
            cells[chunk, below : below + count] = pltpu.matmul_pop(acc).astype(jnp.bfloat16)


def planes_kernel(plan, spec_ref, index_ref, bank_ref, plane, cells, tables, pick, win1, win2, lhs, win, win3, *refs):
    bases, bases3, plane3, bank, index, zeros, sized, in_sems, send_sem, recv_sems, ready = refs
    wins = (win, win1, win2, win3)
    rows, taps, size, cols, owners = plan.rows, plan.taps, plan.granule, plan.cols, plan.owners
    parts = len(RATIOS)
    me = lax.axis_index("freq")

    fetch_own = pltpu.make_async_copy(spec_ref, win.at[:, size : size + cols], in_sems.at[0])
    fetch_own.start()
    fetch_index = pltpu.make_async_copy(index_ref, index, in_sems.at[1])
    fetch_index.start()
    fetch_bank = [
        pltpu.make_async_copy(bank_ref.at[:, :, slab * LANES : (slab + 1) * LANES], bank.at[slab], in_sems.at[2 + slab])
        for slab in range(taps // LANES)
    ]
    run([fetch.start for fetch in fetch_bank])
    barrier = pltpu.get_barrier_semaphore()

    def signal(semaphore, peer):
        pl.semaphore_signal(semaphore, inc=1, device_id={"freq": peer}, device_id_type=pl.DeviceIdType.MESH)

    def greet(k):
        for peer in plan.sources(k, False) + plan.targets(k, True):
            signal(barrier, peer)

    choose(me, 0, owners, greet)
    zeros[...] = jnp.zeros(zeros.shape, zeros.dtype)

    def send(k, far):
        for part, to, begin, count, place in plan.sends(k):
            source = win.at[:, size * (1 + begin) : size * (1 + begin + count)]
            target = wins[part].at[:, size * place : size * (place + count)]
            if to == k:
                if not far:
                    pltpu.make_async_copy(source, target, recv_sems.at[part]).start()
            elif plan.far(k, to) == far:
                pltpu.make_async_remote_copy(
                    src_ref=source,
                    dst_ref=target,
                    send_sem=send_sem,
                    recv_sem=recv_sems.at[part],
                    device_id={"freq": to},
                    device_id_type=pl.DeviceIdType.MESH,
                ).start()

    def fill(part, spot):
        pltpu.make_async_copy(zeros, wins[part].at[:, spot : spot + size], recv_sems.at[part]).start()

    def first(k):
        count = len(plan.targets(k, False)) + len(plan.sources(k, True))
        if count:
            pl.semaphore_wait(barrier, count)
        send(k, False)
        for peer in plan.sources(k, True):
            signal(ready, peer)
        if k == 0:
            for part in range(parts):
                fill(part, 0)
        if k == owners - 1:
            fill(0, size + cols)

    def second(k):
        count = len(plan.targets(k, True))
        if count:
            pl.semaphore_wait(ready, count)
            send(k, True)

    def third(k):
        total = sum(count for _, to, _, count, _ in plan.sends(k) if to != k)
        if total:
            whole = sized.at[:, : total * size]
            pltpu.make_async_copy(whole, whole, send_sem).wait()

    def receive(part):
        whole = sized.at[:, : 2 * size if part == 0 else plan.part_cols[part] + taps]
        pltpu.make_async_copy(whole, whole, recv_sems.at[part]).wait()

    blocks = (cols + taps) // LANES
    halo = size // LANES
    chunks = cols // CHUNK
    tiles = taps // CHUNK
    low, high = size // CHUNK, (size + cols) // CHUNK - 1

    spread = Spread(plan)
    spread.prepare(tables, pick, cells)
    fetch_own.wait()
    choose(me, 0, owners, first)
    fetch_index.wait()
    run([fetch.wait for fetch in fetch_bank])
    fill_bases(win, bases, halo, blocks - halo)
    names = lax.broadcasted_iota(jnp.int32, (bank.shape[2], rows), 0)
    picks = (names == index[...]).astype(jnp.float32).T.astype(jnp.bfloat16)

    def gather(*accs):
        drive(
            [
                [
                    (
                        lambda deep=deep, wide=wide, unit=unit: jnp.concatenate(
                            [
                                bank[wide * CHUNK // LANES + at, unit, deep * CHUNK : (deep + 1) * CHUNK]
                                for at in range(CHUNK // LANES)
                            ],
                            1,
                        ),
                        [(accs[unit * tiles + wide], lambda deep=deep: picks[:, deep * CHUNK : (deep + 1) * CHUNK])],
                    )
                    for wide in range(tiles)
                    for deep in range(bank.shape[2] // CHUNK)
                ]
                for unit in (0, 1)
            ],
        )
        slabs = taps // LANES
        for tile in range(tiles):
            real = pltpu.matmul_pop(accs[tile]).astype(jnp.bfloat16)
            imag = pltpu.matmul_pop(accs[tiles + tile]).astype(jnp.bfloat16)
            for at in range(0, CHUNK, LANES):
                slab, piece = (tile * CHUNK + at) // LANES, slice(at, at + LANES)
                lhs[slab, :rows] = real[:, piece]
                lhs[slab, rows:] = imag[:, piece]
                lhs[slabs + slab, :rows] = -imag[:, piece]
                lhs[slabs + slab, rows:] = real[:, piece]

    pl.run_scoped(gather, *units([rows] * tiles))
    inner = [chunk for chunk in range(chunks) if low <= chunk and chunk + tiles <= high]
    order = [chunk for chunk in range(chunks) if chunk not in inner] + inner

    def split(accs, chosen, shifts, count, spots):
        each = len(accs) // 2
        sides = [dict(zip(chosen, accs[unit * each : (unit + 1) * each])) for unit in (0, 1)]
        queues = [
            taps_queue(lhs, shifts, (rows * unit,), count, side, tiles, (0, 1), spots)
            for unit, side in enumerate(sides)
        ]
        return sides, queues

    def part0(*accs):
        def keep(sides, chunk):
            found = power(*[pltpu.matmul_pop(side[chunk]) for side in sides])
            plane[:, chunk * CHUNK : (chunk + 1) * CHUNK] = found

        sides, queues = split(accs, order, Shifts(bases), rows, range(low, high))
        drive(queues)
        for chunk in inner:
            keep(sides, chunk)
        choose(me, 0, owners, second)
        receive(0)
        receive(3)
        fill_bases(win, bases, 0, halo + 1, 1)
        fill_bases(win, bases, blocks - halo - 1, blocks)
        fill_bases(win3, bases3, 0, (plan.part_cols[3] + taps) // LANES)
        rest = [spot for spot in range(chunks + tiles - 1) if not low <= spot < high]
        sides, queues = split(accs, order, Shifts(bases), rows, rest)
        drive(queues)
        for chunk in order[: chunks - len(inner)]:
            keep(sides, chunk)

    pl.run_scoped(part0, *units([rows] * chunks))
    count3 = plan.part_rows[3]
    number3 = plan.part_cols[3] // CHUNK

    def part3(*accs):
        each = len(accs) // 2
        accs = accs[1:each] + accs[each + 1 :]
        sides, queues = split(accs, range(number3), Shifts(bases3), count3, range(number3 + tiles - 1))
        drive(queues)
        for chunk in range(number3):
            found = power(*[pltpu.matmul_pop(side[chunk]) for side in sides])
            plane3[:, chunk * CHUNK : (chunk + 1) * CHUNK] = found

    pl.run_scoped(part3, *units([rows * chunks - count3 * number3] + [count3] * number3))

    def spread3(*accs):
        drive(spread.queues(3, plane3, tables, accs))
        spread.drain(3, accs, cells)

    pl.run_scoped(spread3, *units([count3] * (chunks // 2)))
    choose(me, 0, owners, third)
    receive(1)
    receive(2)


def sum_kernel(plan, plane, before, tables, pick, win1, win2, lhs, out_ref, out, cells, plane1, plane2, *refs):
    bases1, bases2, sems = refs
    chunks, taps = plan.cols // CHUNK, plan.taps
    tiles = taps // CHUNK
    spread = Spread(plan)
    below = spread.belows[3]
    count1, count2 = plan.part_rows[1], plan.part_rows[2]
    number1, number2 = plan.part_cols[1] // CHUNK, plan.part_cols[2] // CHUNK

    def put(chunk):
        spot = slice(chunk * CHUNK, (chunk + 1) * CHUNK)
        return pltpu.make_async_copy(out.at[:, spot], out_ref.at[:, spot], sems.at[chunk])

    def fill(count, bases, sides):
        number = len(sides[0])
        shifts = Shifts(bases)
        return [
            taps_queue(
                lhs, shifts, (0, plan.rows), count, dict(enumerate(side)), tiles, (unit,), range(number + tiles - 1)
            )
            for unit, side in enumerate(sides)
        ]

    def keep(into, sides):
        count = into.shape[0]
        for chunk, (left, right) in enumerate(zip(*sides)):
            both = pltpu.matmul_pop(left) + pltpu.matmul_pop(right)
            into[:, chunk * CHUNK : (chunk + 1) * CHUNK] = power(both[:count], both[count:])

    def parts(*accs):
        each = len(accs) // 2
        sides = [accs[:each], accs[each:]]
        sides2 = [side[:number2] for side in sides]
        sides1 = [side[number2 : number2 + number1] for side in sides]
        spreads = [acc for side in sides for acc in side[number2 + number1 :]]
        fill_bases(win2, bases2, 0, (plan.part_cols[2] + taps) // LANES)
        fill_bases(win1, bases1, 0, (plan.part_cols[1] + taps) // LANES)
        drive(fill(count2, bases2, sides2))
        keep(plane2, sides2)
        stretches = spread.queues(2, plane2, tables, spreads)
        drive([queue + stretch for queue, stretch in zip(fill(count1, bases1, sides1), stretches)])
        keep(plane1, sides1)
        spread.drain(2, spreads, cells)

    pl.run_scoped(parts, *units([2 * count2] * number2 + [2 * count1] * number1 + [count2] * (chunks // 2)))
    for chunk in range(chunks):
        cells[chunk, below:] = before[chunk, below:]

    def total(*accs):
        each = len(accs) // 2
        half = chunks // 2
        spreads = [acc for unit in (0, 1) for acc in accs[unit * each : unit * each + half]]
        totals = [accs[chunk % 2 * each + half + chunk // 2] for chunk in range(chunks)]
        drive(spread.queues(1, plane1, tables, spreads))
        spread.drain(1, spreads, cells)
        drive(
            [
                [
                    (lambda chunk=chunk: cells[chunk], [(totals[chunk], lambda: pick[...])])
                    for chunk in range(unit, chunks, 2)
                ]
                for unit in (0, 1)
            ]
        )
        for chunk in range(chunks):
            spot = slice(chunk * CHUNK, (chunk + 1) * CHUNK)
            out[:, spot] = plane[:, spot].astype(jnp.float32) + pltpu.matmul_pop(totals[chunk])
            put(chunk).start()

    pl.run_scoped(total, *units([count1] * (chunks // 2) + [plan.rows] * (chunks // 2)))
    for chunk in range(chunks):
        put(chunk).wait()


def body(spectrum, template_bank, template_index):
    owners = lax.axis_size("freq")
    taps = template_bank.shape[2]
    rows = template_index.shape[0]
    cols = spectrum.shape[1]
    plan = Plan(cols, taps, rows, owners)
    hbm = pl.BlockSpec(memory_space=pltpu.HBM)
    vmem = pl.BlockSpec(memory_space=pltpu.VMEM)
    wide = [width + taps for width in plan.part_cols]

    def held(*shape, kind=jnp.bfloat16):
        return pltpu.VMEM(shape, kind)

    between = (
        held(rows, cols),
        held(cols // CHUNK, CHUNK, CHUNK),
        held(len(Spread(plan).tables), CHUNK, CHUNK),
        held(rows, CHUNK),
        held(2, wide[1]),
        held(2, wide[2]),
        held(2 * taps // LANES, 2 * rows, LANES),
    )
    inputs = (spectrum, template_index.reshape(1, rows), template_bank)
    results = pl.pallas_call(
        functools.partial(planes_kernel, plan),
        out_shape=between,
        in_specs=[hbm] * 3,
        out_specs=(vmem,) * len(between),
        scratch_shapes=[
            held(2, wide[0]),
            held(2, wide[3]),
            *[held(2, wide[part] // LANES, TILE, LANES) for part in (0, 3)],
            held(plan.part_rows[3], plan.part_cols[3]),
            held(taps // LANES, *template_bank.shape[:2], LANES),
            held(1, rows, kind=jnp.int32),
            held(2, plan.granule),
            held(2, max(plan.granule * plan.most, *wide)),
            pltpu.SemaphoreType.DMA((2 + taps // LANES,)),
            pltpu.SemaphoreType.DMA,
            pltpu.SemaphoreType.DMA((len(RATIOS),)),
            pltpu.SemaphoreType.REGULAR,
        ],
        compiler_params=pltpu.CompilerParams(collective_id=0, has_side_effects=True, vmem_limit_bytes=24 * 2**20),
        name="planes",
    )(*[pltpu.with_memory_space_constraint(x, pltpu.HBM) for x in inputs])
    return pl.pallas_call(
        functools.partial(sum_kernel, plan),
        out_shape=jax.ShapeDtypeStruct((rows, cols), jnp.float32),
        in_specs=[vmem] * len(between),
        out_specs=hbm,
        scratch_shapes=[
            held(rows, cols, kind=jnp.float32),
            held(cols // CHUNK, CHUNK, CHUNK),
            *[held(plan.part_rows[part], plan.part_cols[part]) for part in (1, 2)],
            *[held(2, wide[part] // LANES, TILE, LANES) for part in (1, 2)],
            pltpu.SemaphoreType.DMA((cols // CHUNK,)),
        ],
        compiler_params=pltpu.CompilerParams(vmem_limit_bytes=24 * 2**20),
        name="sums",
    )(*results)


def solution(mesh):
    return jax.shard_map(
        body,
        mesh=mesh,
        in_specs=(P(None, ("beam", "freq")), P(), P()),
        out_specs=P(None, ("beam", "freq")),
        check_vma=False,
    )
```

```python
import functools

import jax
import jax.numpy as jnp
from jax import lax
from jax.experimental import pallas as pl
from jax.experimental.pallas import tpu as pltpu
from jax.sharding import PartitionSpec as P

RATIOS = ((1, 1), (1, 2), (1, 4), (3, 4))
CHUNK = 256
LANES = 128
TILE = 16


class Plan:
    def __init__(self, cols, taps, rows, owners):
        self.cols, self.taps, self.rows, self.owners = cols, taps, rows, owners
        self.granule = taps // 2
        self.held = cols // self.granule
        self.steps = [self.held * n // d for n, d in RATIOS]
        self.part_cols = [cols * n // d for n, d in RATIOS]
        self.part_rows = [rows * n // d for n, d in RATIOS]
        self.most = max(sum(count for _, _, _, count, _ in self.sends(source)) for source in range(owners))

    def pieces(self, source, target):
        found = []
        for part, step in enumerate(self.steps):
            first = step * target - 1
            low = max(self.held * source, first)
            high = min(self.held * (source + 1), first + step + 2)
            if low < high and (part or source != target):
                found.append((part, target, low - self.held * source, high - low, low - first))
        return found

    def sends(self, source):
        near = range(max(0, source - 1), min(self.owners, 4 * source + 8))
        return [piece for target in near for piece in self.pieces(source, target)]

    def far(self, source, target):
        return not any(part in (0, len(RATIOS) - 1) for part, *_ in self.pieces(source, target))

    def targets(self, me, far):
        return [to for to in range(self.owners) if to != me and self.far(me, to) == far and self.pieces(me, to)]

    def sources(self, me, far):
        return [by for by in range(self.owners) if by != me and self.far(by, me) == far and self.pieces(by, me)]


def choose(me, low, high, act):
    if high - low == 1:
        act(low)
    else:
        middle = (low + high) // 2
        pl.when(me < middle)(lambda: choose(me, low, middle, act))
        pl.when(me >= middle)(lambda: choose(me, middle, high, act))


def one_hot(shape, make):
    left = lax.broadcasted_iota(jnp.int32, shape, 0)
    right = lax.broadcasted_iota(jnp.int32, shape, 1)
    return make(left, right).astype(jnp.float32).astype(jnp.bfloat16)


def fill_bases(window, bases, low, high, spare=0):
    width = (high - low) * LANES
    for which in (0, 1):
        line = window[which : which + 1, low * LANES : high * LANES].astype(jnp.float32)
        base = jnp.broadcast_to(line, (8, width))
        place = lax.broadcasted_iota(jnp.int32, (8, width), 0)
        for bit in (1, 2, 4):
            base = jnp.where((place & bit) != 0, pltpu.roll(base, width - bit, 1), base)
        base = jnp.concatenate([base, pltpu.roll(base, width - 8, 1)], 0).astype(jnp.bfloat16)
        for block in range(low, high - spare):
            bases[which, block] = base[:, (block - low) * LANES : (block - low + 1) * LANES]


class Shifts:
    def __init__(self, bases):
        self.bases = bases
        self.turned, self.blocks = {}, {}
        lane = lax.broadcasted_iota(jnp.int32, (TILE, LANES), 1)
        self.keep = [lane < LANES - TILE * turn for turn in range(LANES // TILE)]

    def turn(self, which, block, turn):
        key = which, block, turn
        if key not in self.turned:
            value = self.bases[which, block]
            self.turned[key] = pltpu.roll(value, LANES - TILE * turn, 1) if turn else value
        return self.turned[key]

    def block(self, which, block):
        key = which, block
        if key not in self.blocks:
            rows = [self.turn(which, block, 0)]
            for turn in range(1, LANES // TILE):
                rows.append(
                    jnp.where(self.keep[turn], self.turn(which, block, turn), self.turn(which, block + 1, turn))
                )
            self.blocks[key] = jnp.concatenate(rows, 0)
        return self.blocks[key]

    def tile(self, which, spot):
        each = CHUNK // LANES
        return jnp.concatenate(
            [
                jnp.concatenate([self.block(which, each * spot + at + row) for row in range(each)], 0)
                for at in range(each)
            ],
            1,
        )


def run(tasks):
    for task in tasks:
        task()


def rows_of(lhs, first, count, which, tile):
    half = lhs.shape[0] // 2
    each = CHUNK // LANES
    slabs = [which * half + each * tile + at for at in range(each)]
    return jnp.concatenate(
        [jnp.concatenate([lhs[slab, row : row + count] for row in first], 0) for slab in slabs], 1
    )


def drive(queues):
    longest = max(len(queue) for queue in queues)
    for step in range(longest + 1):
        for unit, queue in enumerate(queues):
            if step < len(queue):
                pltpu.matmul_push_rhs(queue[step][0](), staging_register=step % 2, mxu_index=unit)
        for unit, queue in enumerate(queues):
            if 0 < step <= len(queue):
                for number, (acc, rows) in enumerate(queue[step - 1][1]):
                    pltpu.matmul_acc_lhs(acc, rows(), load_staged_rhs=None if number else (step - 1) % 2)


def taps_queue(lhs, shifts, first, count, accs, tiles, kinds, spots):
    return [
        (
            functools.partial(shifts.tile, which, spot),
            [
                (acc, functools.partial(rows_of, lhs, first, count, which, spot - chunk))
                for chunk, acc in accs.items()
                if 0 <= spot - chunk < tiles
            ],
        )
        for which in kinds
        for spot in spots
    ]


def power(real, imag):
    return (real * real + imag * imag).astype(jnp.bfloat16)


def units(shapes):
    return [pltpu.ACC(unit)((rows, CHUNK), jnp.float32) for unit in (0, 1) for rows in shapes]


class Spread:
    def __init__(self, plan):
        self.plan = plan
        self.chunks = plan.cols // CHUNK
        self.belows = [sum(plan.part_rows[1:part]) for part in range(len(RATIOS))]
        self.used = sum(plan.part_rows[1:])
        self.tables = sorted(
            {(part, self.place(part, chunk)[1]) for part in range(1, len(RATIOS)) for chunk in range(self.chunks)}
        )

    def place(self, part, chunk):
        start = CHUNK * RATIOS[part][0] // RATIOS[part][1] * chunk
        base = min(start // LANES * LANES, self.plan.part_cols[part] - CHUNK)
        return base, start - base

    def prepare(self, tables, pick):
        for number, (part, skip) in enumerate(self.tables):
            n, d = RATIOS[part]
            tables[number] = one_hot((CHUNK, CHUNK), lambda k, r: k == skip + r * n // d)
        left = lax.broadcasted_iota(jnp.int32, pick.shape, 0)
        right = lax.broadcasted_iota(jnp.int32, pick.shape, 1)
        hits = [right == self.belows[part] + left * n // d for part, (n, d) in enumerate(RATIOS) if part]
        pick[...] = functools.reduce(jnp.logical_or, hits).astype(jnp.float32).astype(jnp.bfloat16)

    def queues(self, part, plane, tables, accs):
        half = self.chunks // 2
        found = []
        for unit in (0, 1):
            mine = list(range(unit, self.chunks, 2))
            queue = []
            for skip in sorted({self.place(part, chunk)[1] for chunk in mine}):
                number = self.tables.index((part, skip))
                users = []
                for chunk in mine:
                    base, skipped = self.place(part, chunk)
                    if skipped == skip:
                        users.append((accs[unit * half + chunk // 2], lambda base=base: plane[:, base : base + CHUNK]))
                queue.append((lambda number=number: tables[number], users))
            found.append(queue)
        return found

    def drain(self, part, accs, cells):
        count, below = self.plan.part_rows[part], self.belows[part]
        for chunk in range(self.chunks):
            acc = accs[chunk % 2 * (self.chunks // 2) + chunk // 2]
            cells[chunk, below : below + count] = pltpu.matmul_pop(acc).astype(jnp.bfloat16)


def planes_kernel(plan, spec_ref, index_ref, bank_ref, plane, plane3, tables, pick, win1, win2, lhs, win, win3, *refs):
    bases, bases3, bank, index, zeros, sized, in_sems, send_sem, recv_sems, ready = refs
    wins = (win, win1, win2, win3)
    rows, taps, size, cols, owners = plan.rows, plan.taps, plan.granule, plan.cols, plan.owners
    parts = len(RATIOS)
    me = lax.axis_index("freq")

    fetch_own = pltpu.make_async_copy(spec_ref, win.at[:, size : size + cols], in_sems.at[0])
    fetch_own.start()
    fetch_index = pltpu.make_async_copy(index_ref, index, in_sems.at[1])
    fetch_index.start()
    fetch_bank = [
        pltpu.make_async_copy(bank_ref.at[:, :, slab * LANES : (slab + 1) * LANES], bank.at[slab], in_sems.at[2 + slab])
        for slab in range(taps // LANES)
    ]
    run([fetch.start for fetch in fetch_bank])
    barrier = pltpu.get_barrier_semaphore()

    def signal(semaphore, peer):
        pl.semaphore_signal(semaphore, inc=1, device_id={"freq": peer}, device_id_type=pl.DeviceIdType.MESH)

    def greet(k):
        for peer in plan.sources(k, False) + plan.targets(k, True):
            signal(barrier, peer)

    choose(me, 0, owners, greet)
    zeros[...] = jnp.zeros(zeros.shape, zeros.dtype)

    def send(k, far):
        for part, to, begin, count, place in plan.sends(k):
            source = win.at[:, size * (1 + begin) : size * (1 + begin + count)]
            target = wins[part].at[:, size * place : size * (place + count)]
            if to == k:
                if not far:
                    pltpu.make_async_copy(source, target, recv_sems.at[part]).start()
            elif plan.far(k, to) == far:
                pltpu.make_async_remote_copy(
                    src_ref=source,
                    dst_ref=target,
                    send_sem=send_sem,
                    recv_sem=recv_sems.at[part],
                    device_id={"freq": to},
                    device_id_type=pl.DeviceIdType.MESH,
                ).start()

    def fill(part, spot):
        pltpu.make_async_copy(zeros, wins[part].at[:, spot : spot + size], recv_sems.at[part]).start()

    def first(k):
        count = len(plan.targets(k, False)) + len(plan.sources(k, True))
        if count:
            pl.semaphore_wait(barrier, count)
        for peer in plan.sources(k, True):
            signal(ready, peer)
        send(k, False)
        if k == 0:
            for part in range(parts):
                fill(part, 0)
        if k == owners - 1:
            fill(0, size + cols)

    def second(k):
        count = len(plan.targets(k, True))
        if count:
            pl.semaphore_wait(ready, count)
            send(k, True)

    def third(k):
        total = sum(count for _, to, _, count, _ in plan.sends(k) if to != k)
        if total:
            whole = sized.at[:, : total * size]
            pltpu.make_async_copy(whole, whole, send_sem).wait()

    def receive(part):
        whole = sized.at[:, : 2 * size if part == 0 else plan.part_cols[part] + taps]
        pltpu.make_async_copy(whole, whole, recv_sems.at[part]).wait()

    blocks = (cols + taps) // LANES
    halo = size // LANES
    chunks = cols // CHUNK
    tiles = taps // CHUNK
    low, high = size // CHUNK, (size + cols) // CHUNK - 1

    spread = Spread(plan)
    spread.prepare(tables, pick)
    fetch_index.wait()
    names = lax.broadcasted_iota(jnp.int32, (bank.shape[2], rows), 0)
    picks = (names == index[...]).astype(jnp.float32).T.astype(jnp.bfloat16)
    fetch_own.wait()
    fill_bases(win, bases, halo, blocks - halo)
    choose(me, 0, owners, first)
    run([fetch.wait for fetch in fetch_bank])

    def gather(*accs):
        drive(
            [
                [
                    (
                        lambda deep=deep, wide=wide, unit=unit: jnp.concatenate(
                            [
                                bank[wide * CHUNK // LANES + at, unit, deep * CHUNK : (deep + 1) * CHUNK]
                                for at in range(CHUNK // LANES)
                            ],
                            1,
                        ),
                        [(accs[unit * tiles + wide], lambda deep=deep: picks[:, deep * CHUNK : (deep + 1) * CHUNK])],
                    )
                    for wide in range(tiles)
                    for deep in range(bank.shape[2] // CHUNK)
                ]
                for unit in (0, 1)
            ],
        )
        slabs = taps // LANES
        for tile in range(tiles):
            real = pltpu.matmul_pop(accs[tile]).astype(jnp.bfloat16)
            imag = pltpu.matmul_pop(accs[tiles + tile]).astype(jnp.bfloat16)
            for at in range(0, CHUNK, LANES):
                slab, piece = (tile * CHUNK + at) // LANES, slice(at, at + LANES)
                lhs[slab, :rows] = real[:, piece]
                lhs[slab, rows:] = imag[:, piece]
                lhs[slabs + slab, :rows] = -imag[:, piece]
                lhs[slabs + slab, rows:] = real[:, piece]

    pl.run_scoped(gather, *units([rows] * tiles))
    inner = [chunk for chunk in range(chunks) if low <= chunk and chunk + tiles <= high]

    def split(sides, base, count, chosen):
        return [
            taps_queue(lhs, Shifts(base), (0, rows), count, side, tiles, (0, 1), [spot for spot in spots if chosen(spot)])
            for side in sides
            for spots in [range(min(side), max(side) + tiles)]
        ]

    def sided(accs, number):
        each = len(accs) // 2
        sides = []
        for unit in (0, 1):
            mine = range(unit * number // 2, (unit + 1) * number // 2)
            if number == chunks:
                mine = sorted(mine, key=lambda chunk: chunk in inner)
            sides.append(dict(zip(mine, accs[unit * each + each - len(mine) : (unit + 1) * each])))
        return sides

    def keep(into, sides, chosen):
        count = into.shape[0]
        for side in sides:
            for chunk in sorted(side):
                if chunk in chosen:
                    both = pltpu.matmul_pop(side[chunk])
                    into[:, chunk * CHUNK : (chunk + 1) * CHUNK] = power(both[:count], both[count:])

    def part0(*accs):
        sides = sided(accs, chunks)
        drive(split(sides, bases, rows, lambda spot: low <= spot < high))
        keep(plane, sides, inner)
        receive(0)
        receive(3)
        fill_bases(win, bases, 0, halo + 1, 1)
        fill_bases(win, bases, blocks - halo - 1, blocks)
        drive(split(sides, bases, rows, lambda spot: not low <= spot < high))
        fill_bases(win3, bases3, 0, (plan.part_cols[3] + taps) // LANES)
        keep(plane, sides, [chunk for chunk in range(chunks) if chunk not in inner])

    pl.run_scoped(part0, *units([2 * rows] * (chunks // 2)))
    choose(me, 0, owners, second)
    count3 = plan.part_rows[3]
    number3 = plan.part_cols[3] // CHUNK

    def part3(*accs):
        sides = sided(accs, number3)
        drive(split(sides, bases3, count3, lambda spot: True))
        keep(plane3, sides, range(number3))

    pl.run_scoped(part3, *units([2 * count3] * (number3 // 2)))

    choose(me, 0, owners, third)
    receive(1)
    receive(2)


def sum_kernel(plan, plane, plane3, tables, pick, win1, win2, lhs, out_ref, out, cells, plane1, plane2, *refs):
    bases1, bases2, sems = refs
    chunks, taps = plan.cols // CHUNK, plan.taps
    tiles = taps // CHUNK
    spread = Spread(plan)
    count1, count2 = plan.part_rows[1], plan.part_rows[2]
    number1, number2 = plan.part_cols[1] // CHUNK, plan.part_cols[2] // CHUNK

    def put(chunk):
        spot = slice(chunk * CHUNK, (chunk + 1) * CHUNK)
        return pltpu.make_async_copy(out.at[:, spot], out_ref.at[:, spot], sems.at[chunk])

    def fill(count, bases, sides):
        number = len(sides[0])
        shifts = Shifts(bases)
        return [
            taps_queue(
                lhs, shifts, (0, plan.rows), count, dict(enumerate(side)), tiles, (unit,), range(number + tiles - 1)
            )
            for unit, side in enumerate(sides)
        ]

    def keep(into, sides):
        count = into.shape[0]
        for chunk, (left, right) in enumerate(zip(*sides)):
            both = pltpu.matmul_pop(left) + pltpu.matmul_pop(right)
            into[:, chunk * CHUNK : (chunk + 1) * CHUNK] = power(both[:count], both[count:])

    half = chunks // 2

    def halves(accs, sizes):
        each = len(accs) // 2
        groups, at = [], 0
        for size in sizes:
            groups.append([accs[unit * each + at : unit * each + at + size] for unit in (0, 1)])
            at += size
        return groups

    def flat(sides):
        return [acc for side in sides for acc in side]

    for chunk in range(chunks):
        cells[chunk, spread.used :] = jnp.zeros((CHUNK - spread.used, CHUNK), cells.dtype)

    def parts(*accs):
        sides2, sides1, spreads = halves(accs, (number2, number1, half))
        fill_bases(win2, bases2, 0, (plan.part_cols[2] + taps) // LANES)
        fill_bases(win1, bases1, 0, (plan.part_cols[1] + taps) // LANES)
        queues = zip(
            spread.queues(3, plane3, tables, flat(spreads)),
            fill(count2, bases2, sides2),
            fill(count1, bases1, sides1),
        )
        drive([sum(queue, []) for queue in queues])
        spread.drain(3, flat(spreads), cells)
        keep(plane2, sides2)
        keep(plane1, sides1)

    pl.run_scoped(parts, *units([2 * count2] * number2 + [2 * count1] * number1 + [plan.part_rows[3]] * half))

    def total(*accs):
        spreads2, spreads1, sides = halves(accs, (half, half, half))
        totals = [sides[chunk % 2][chunk // 2] for chunk in range(chunks)]
        queues = zip(
            spread.queues(2, plane2, tables, flat(spreads2)),
            spread.queues(1, plane1, tables, flat(spreads1)),
        )
        drive([sum(queue, []) for queue in queues])
        spread.drain(2, flat(spreads2), cells)
        spread.drain(1, flat(spreads1), cells)
        drive(
            [
                [
                    (lambda chunk=chunk: cells[chunk], [(totals[chunk], lambda: pick[...])])
                    for chunk in range(unit, chunks, 2)
                ]
                for unit in (0, 1)
            ]
        )
        for chunk in range(chunks):
            spot = slice(chunk * CHUNK, (chunk + 1) * CHUNK)
            out[:, spot] = plane[:, spot].astype(jnp.float32) + pltpu.matmul_pop(totals[chunk])
            put(chunk).start()

    pl.run_scoped(total, *units([count2] * half + [count1] * half + [plan.rows] * half))
    for chunk in range(chunks):
        put(chunk).wait()


def body(spectrum, template_bank, template_index):
    owners = lax.axis_size("freq")
    taps = template_bank.shape[2]
    rows = template_index.shape[0]
    cols = spectrum.shape[1]
    plan = Plan(cols, taps, rows, owners)
    hbm = pl.BlockSpec(memory_space=pltpu.HBM)
    vmem = pl.BlockSpec(memory_space=pltpu.VMEM)
    wide = [width + taps for width in plan.part_cols]

    def held(*shape, kind=jnp.bfloat16):
        return pltpu.VMEM(shape, kind)

    between = (
        held(rows, cols),
        held(plan.part_rows[3], plan.part_cols[3]),
        held(len(Spread(plan).tables), CHUNK, CHUNK),
        held(rows, CHUNK),
        held(2, wide[1]),
        held(2, wide[2]),
        held(2 * taps // LANES, 2 * rows, LANES),
    )
    inputs = (spectrum, template_index.reshape(1, rows), template_bank)
    results = pl.pallas_call(
        functools.partial(planes_kernel, plan),
        out_shape=between,
        in_specs=[hbm] * 3,
        out_specs=(vmem,) * len(between),
        scratch_shapes=[
            held(2, wide[0]),
            held(2, wide[3]),
            *[held(2, wide[part] // LANES, TILE, LANES) for part in (0, 3)],
            held(taps // LANES, *template_bank.shape[:2], LANES),
            held(1, rows, kind=jnp.int32),
            held(2, plan.granule),
            held(2, max(plan.granule * plan.most, *wide)),
            pltpu.SemaphoreType.DMA((2 + taps // LANES,)),
            pltpu.SemaphoreType.DMA,
            pltpu.SemaphoreType.DMA((len(RATIOS),)),
            pltpu.SemaphoreType.REGULAR,
        ],
        compiler_params=pltpu.CompilerParams(collective_id=0, has_side_effects=True, vmem_limit_bytes=24 * 2**20),
        name="planes",
    )(*[pltpu.with_memory_space_constraint(x, pltpu.HBM) for x in inputs])
    return pl.pallas_call(
        functools.partial(sum_kernel, plan),
        out_shape=jax.ShapeDtypeStruct((rows, cols), jnp.float32),
        in_specs=[vmem] * len(between),
        out_specs=hbm,
        scratch_shapes=[
            held(rows, cols, kind=jnp.float32),
            held(cols // CHUNK, CHUNK, CHUNK),
            *[held(plan.part_rows[part], plan.part_cols[part]) for part in (1, 2)],
            *[held(2, wide[part] // LANES, TILE, LANES) for part in (1, 2)],
            pltpu.SemaphoreType.DMA((cols // CHUNK,)),
        ],
        compiler_params=pltpu.CompilerParams(vmem_limit_bytes=24 * 2**20),
        name="sums",
    )(*results)


def solution(mesh):
    return jax.shard_map(
        body,
        mesh=mesh,
        in_specs=(P(None, ("beam", "freq")), P(), P()),
        out_specs=P(None, ("beam", "freq")),
        check_vma=False,
    )
```

```python
import functools

import jax
import jax.numpy as jnp
from jax import lax
from jax.experimental import pallas as pl
from jax.experimental.pallas import tpu as pltpu
from jax.sharding import PartitionSpec as P

RATIOS = ((1, 1), (1, 2), (1, 4), (3, 4))
CHUNK = 256
LANES = 128
TILE = 16


class Plan:
    def __init__(self, cols, taps, rows, owners):
        self.cols, self.taps, self.rows, self.owners = cols, taps, rows, owners
        self.granule = taps // 2
        self.held = cols // self.granule
        self.steps = [self.held * n // d for n, d in RATIOS]
        self.part_cols = [cols * n // d for n, d in RATIOS]
        self.part_rows = [rows * n // d for n, d in RATIOS]
        self.most = max(sum(count for _, _, _, count, _ in self.sends(source)) for source in range(owners))

    def pieces(self, source, target):
        found = []
        for part, step in enumerate(self.steps):
            first = step * target - 1
            low = max(self.held * source, first)
            high = min(self.held * (source + 1), first + step + 2)
            if low < high and (part or source != target):
                found.append((part, target, low - self.held * source, high - low, low - first))
        return found

    def sends(self, source):
        near = range(max(0, source - 1), min(self.owners, 4 * source + 8))
        return [piece for target in near for piece in self.pieces(source, target)]

    def far(self, source, target):
        return not any(part in (0, len(RATIOS) - 1) for part, *_ in self.pieces(source, target))

    def targets(self, me, far):
        return [to for to in range(self.owners) if to != me and self.far(me, to) == far and self.pieces(me, to)]

    def sources(self, me, far):
        return [by for by in range(self.owners) if by != me and self.far(by, me) == far and self.pieces(by, me)]


def choose(me, low, high, act):
    if high - low == 1:
        act(low)
    else:
        middle = (low + high) // 2
        pl.when(me < middle)(lambda: choose(me, low, middle, act))
        pl.when(me >= middle)(lambda: choose(me, middle, high, act))


def one_hot(shape, make):
    left = lax.broadcasted_iota(jnp.int32, shape, 0)
    right = lax.broadcasted_iota(jnp.int32, shape, 1)
    return make(left, right).astype(jnp.float32).astype(jnp.bfloat16)


def fill_bases(window, bases, low, high, spare=0):
    width = (high - low) * LANES
    for which in (0, 1):
        line = window[which : which + 1, low * LANES : high * LANES].astype(jnp.float32)
        base = jnp.broadcast_to(line, (8, width))
        place = lax.broadcasted_iota(jnp.int32, (8, width), 0)
        for bit in (1, 2, 4):
            base = jnp.where((place & bit) != 0, pltpu.roll(base, width - bit, 1), base)
        base = jnp.concatenate([base, pltpu.roll(base, width - 8, 1)], 0).astype(jnp.bfloat16)
        for block in range(low, high - spare):
            bases[which, block] = base[:, (block - low) * LANES : (block - low + 1) * LANES]


class Shifts:
    def __init__(self, bases):
        self.bases = bases
        self.turned, self.blocks = {}, {}
        lane = lax.broadcasted_iota(jnp.int32, (TILE, LANES), 1)
        self.keep = [lane < LANES - TILE * turn for turn in range(LANES // TILE)]

    def turn(self, which, block, turn):
        key = which, block, turn
        if key not in self.turned:
            value = self.bases[which, block]
            self.turned[key] = pltpu.roll(value, LANES - TILE * turn, 1) if turn else value
        return self.turned[key]

    def block(self, which, block):
        key = which, block
        if key not in self.blocks:
            rows = [self.turn(which, block, 0)]
            for turn in range(1, LANES // TILE):
                rows.append(
                    jnp.where(self.keep[turn], self.turn(which, block, turn), self.turn(which, block + 1, turn))
                )
            self.blocks[key] = jnp.concatenate(rows, 0)
        return self.blocks[key]

    def tile(self, which, spot):
        each = CHUNK // LANES
        return jnp.concatenate(
            [
                jnp.concatenate([self.block(which, each * spot + at + row) for row in range(each)], 0)
                for at in range(each)
            ],
            1,
        )


def run(tasks):
    for task in tasks:
        task()


def rows_of(lhs, first, count, which, tile):
    half = lhs.shape[0] // 2
    each = CHUNK // LANES
    slabs = [which * half + each * tile + at for at in range(each)]
    return jnp.concatenate(
        [jnp.concatenate([lhs[slab, row : row + count] for row in first], 0) for slab in slabs], 1
    )


def drive(queues):
    longest = max(len(queue) for queue in queues)
    for step in range(longest + 1):
        for unit, queue in enumerate(queues):
            if step < len(queue):
                pltpu.matmul_push_rhs(queue[step][0](), staging_register=step % 2, mxu_index=unit)
        for unit, queue in enumerate(queues):
            if 0 < step <= len(queue):
                for number, (acc, rows) in enumerate(queue[step - 1][1]):
                    pltpu.matmul_acc_lhs(acc, rows(), load_staged_rhs=None if number else (step - 1) % 2)


def taps_queue(lhs, shifts, first, count, accs, tiles, kinds, spots):
    return [
        (
            functools.partial(shifts.tile, which, spot),
            [
                (acc, functools.partial(rows_of, lhs, first, count, which, spot - chunk))
                for chunk, acc in accs.items()
                if 0 <= spot - chunk < tiles
            ],
        )
        for which in kinds
        for spot in spots
    ]


def power(real, imag):
    return (real * real + imag * imag).astype(jnp.bfloat16)


def units(shapes):
    return [pltpu.ACC(unit)((rows, CHUNK), jnp.float32) for unit in (0, 1) for rows in shapes]


class Spread:
    def __init__(self, plan):
        self.plan = plan
        self.chunks = plan.cols // CHUNK
        self.belows = [sum(plan.part_rows[1:part]) for part in range(len(RATIOS))]
        self.used = sum(plan.part_rows[1:])
        self.tables = sorted(
            {(part, self.place(part, chunk)[1]) for part in range(1, len(RATIOS)) for chunk in range(self.chunks)}
        )

    def place(self, part, chunk):
        start = CHUNK * RATIOS[part][0] // RATIOS[part][1] * chunk
        base = min(start // LANES * LANES, self.plan.part_cols[part] - CHUNK)
        return base, start - base

    def prepare(self, tables, pick):
        for number, (part, skip) in enumerate(self.tables):
            n, d = RATIOS[part]
            tables[number] = one_hot((CHUNK, CHUNK), lambda k, r: k == skip + r * n // d)
        left = lax.broadcasted_iota(jnp.int32, pick.shape, 0)
        right = lax.broadcasted_iota(jnp.int32, pick.shape, 1)
        hits = [right == self.belows[part] + left * n // d for part, (n, d) in enumerate(RATIOS) if part]
        pick[...] = functools.reduce(jnp.logical_or, hits).astype(jnp.float32).astype(jnp.bfloat16)

    def queues(self, part, plane, tables, accs):
        half = self.chunks // 2
        found = []
        for unit in (0, 1):
            mine = list(range(unit, self.chunks, 2))
            queue = []
            for skip in sorted({self.place(part, chunk)[1] for chunk in mine}):
                number = self.tables.index((part, skip))
                users = []
                for chunk in mine:
                    base, skipped = self.place(part, chunk)
                    if skipped == skip:
                        users.append((accs[unit * half + chunk // 2], lambda base=base: plane[:, base : base + CHUNK]))
                queue.append((lambda number=number: tables[number], users))
            found.append(queue)
        return found

    def drain(self, part, accs, cells):
        count, below = self.plan.part_rows[part], self.belows[part]
        for chunk in range(self.chunks):
            acc = accs[chunk % 2 * (self.chunks // 2) + chunk // 2]
            cells[chunk, below : below + count] = pltpu.matmul_pop(acc).astype(jnp.bfloat16)


def planes_kernel(plan, spec_ref, index_ref, bank_ref, plane, plane3, tables, pick, win1, win2, lhs, win, win3, *refs):
    bases, bases3, bank, index, zeros, sized, in_sems, send_sem, recv_sems, ready = refs
    wins = (win, win1, win2, win3)
    rows, taps, size, cols, owners = plan.rows, plan.taps, plan.granule, plan.cols, plan.owners
    parts = len(RATIOS)
    me = lax.axis_index("freq")

    fetch_own = pltpu.make_async_copy(spec_ref, win.at[:, size : size + cols], in_sems.at[0])
    fetch_own.start()
    fetch_index = pltpu.make_async_copy(index_ref, index, in_sems.at[1])
    fetch_index.start()
    fetch_bank = [
        pltpu.make_async_copy(bank_ref.at[:, :, slab * LANES : (slab + 1) * LANES], bank.at[slab], in_sems.at[2 + slab])
        for slab in range(taps // LANES)
    ]
    run([fetch.start for fetch in fetch_bank])
    barrier = pltpu.get_barrier_semaphore()

    def signal(semaphore, peer):
        pl.semaphore_signal(semaphore, inc=1, device_id={"freq": peer}, device_id_type=pl.DeviceIdType.MESH)

    def greet(k):
        for peer in plan.sources(k, False) + plan.targets(k, True):
            signal(barrier, peer)

    choose(me, 0, owners, greet)
    zeros[...] = jnp.zeros(zeros.shape, zeros.dtype)

    def send(k, far):
        for part, to, begin, count, place in reversed(plan.sends(k)):
            source = win.at[:, size * (1 + begin) : size * (1 + begin + count)]
            target = wins[part].at[:, size * place : size * (place + count)]
            if to == k:
                if not far:
                    pltpu.make_async_copy(source, target, recv_sems.at[part]).start()
            elif plan.far(k, to) == far:
                pltpu.make_async_remote_copy(
                    src_ref=source,
                    dst_ref=target,
                    send_sem=send_sem,
                    recv_sem=recv_sems.at[part],
                    device_id={"freq": to},
                    device_id_type=pl.DeviceIdType.MESH,
                ).start()

    def fill(part, spot):
        pltpu.make_async_copy(zeros, wins[part].at[:, spot : spot + size], recv_sems.at[part]).start()

    def first(k):
        count = len(plan.targets(k, False)) + len(plan.sources(k, True))
        if count:
            pl.semaphore_wait(barrier, count)
        for peer in plan.sources(k, True):
            signal(ready, peer)
        send(k, False)
        if k == 0:
            for part in range(parts):
                fill(part, 0)
        if k == owners - 1:
            fill(0, size + cols)

    def second(k, early):
        if early != (k >= owners // 8):
            return
        count = len(plan.targets(k, True))
        if count:
            pl.semaphore_wait(ready, count)
            send(k, True)

    def third(k):
        total = sum(count for _, to, _, count, _ in plan.sends(k) if to != k)
        if total:
            whole = sized.at[:, : total * size]
            pltpu.make_async_copy(whole, whole, send_sem).wait()

    def receive(part):
        whole = sized.at[:, : 2 * size if part == 0 else plan.part_cols[part] + taps]
        pltpu.make_async_copy(whole, whole, recv_sems.at[part]).wait()

    blocks = (cols + taps) // LANES
    halo = size // LANES
    chunks = cols // CHUNK
    tiles = taps // CHUNK
    low, high = size // CHUNK, (size + cols) // CHUNK - 1

    spread = Spread(plan)
    spread.prepare(tables, pick)
    fetch_index.wait()
    names = lax.broadcasted_iota(jnp.int32, (bank.shape[2], rows), 0)
    picks = (names == index[...]).astype(jnp.float32).T.astype(jnp.bfloat16)
    fetch_own.wait()
    fill_bases(win, bases, halo, blocks - halo)
    choose(me, 0, owners, first)
    run([fetch.wait for fetch in fetch_bank])

    def gather(*accs):
        drive(
            [
                [
                    (
                        lambda deep=deep, wide=wide, unit=unit: jnp.concatenate(
                            [
                                bank[wide * CHUNK // LANES + at, unit, deep * CHUNK : (deep + 1) * CHUNK]
                                for at in range(CHUNK // LANES)
                            ],
                            1,
                        ),
                        [(accs[unit * tiles + wide], lambda deep=deep: picks[:, deep * CHUNK : (deep + 1) * CHUNK])],
                    )
                    for wide in range(tiles)
                    for deep in range(bank.shape[2] // CHUNK)
                ]
                for unit in (0, 1)
            ],
        )
        slabs = taps // LANES
        for tile in range(tiles):
            real = pltpu.matmul_pop(accs[tile]).astype(jnp.bfloat16)
            imag = pltpu.matmul_pop(accs[tiles + tile]).astype(jnp.bfloat16)
            for at in range(0, CHUNK, LANES):
                slab, piece = (tile * CHUNK + at) // LANES, slice(at, at + LANES)
                lhs[slab, :rows] = real[:, piece]
                lhs[slab, rows:] = imag[:, piece]
                lhs[slabs + slab, :rows] = -imag[:, piece]
                lhs[slabs + slab, rows:] = real[:, piece]

    pl.run_scoped(gather, *units([rows] * tiles))
    inner = [chunk for chunk in range(chunks) if low <= chunk and chunk + tiles <= high]

    def split(sides, base, count, chosen):
        return [
            taps_queue(lhs, Shifts(base), (0, rows), count, side, tiles, (0, 1), [spot for spot in spots if chosen(spot)])
            for side in sides
            for spots in [range(min(side), max(side) + tiles)]
        ]

    def sided(accs, number):
        each = len(accs) // 2
        sides = []
        for unit in (0, 1):
            mine = range(unit * number // 2, (unit + 1) * number // 2)
            if number == chunks:
                mine = sorted(mine, key=lambda chunk: chunk in inner)
            sides.append(dict(zip(mine, accs[unit * each + each - len(mine) : (unit + 1) * each])))
        return sides

    def keep(into, sides, chosen):
        count = into.shape[0]
        for side in sides:
            for chunk in sorted(side):
                if chunk in chosen:
                    both = pltpu.matmul_pop(side[chunk])
                    into[:, chunk * CHUNK : (chunk + 1) * CHUNK] = power(both[:count], both[count:])

    def part0(*accs):
        sides = sided(accs, chunks)
        drive(split(sides, bases, rows, lambda spot: low <= spot < high))
        keep(plane, sides, inner)
        choose(me, 0, owners, functools.partial(second, early=True))
        receive(0)
        receive(3)
        fill_bases(win, bases, 0, halo + 1, 1)
        fill_bases(win, bases, blocks - halo - 1, blocks)
        drive(split(sides, bases, rows, lambda spot: not low <= spot < high))
        fill_bases(win3, bases3, 0, (plan.part_cols[3] + taps) // LANES)
        keep(plane, sides, [chunk for chunk in range(chunks) if chunk not in inner])

    pl.run_scoped(part0, *units([2 * rows] * (chunks // 2)))
    choose(me, 0, owners, functools.partial(second, early=False))
    count3 = plan.part_rows[3]
    number3 = plan.part_cols[3] // CHUNK

    def part3(*accs):
        sides = sided(accs, number3)
        drive(split(sides, bases3, count3, lambda spot: True))
        keep(plane3, sides, range(number3))

    pl.run_scoped(part3, *units([2 * count3] * (number3 // 2)))

    choose(me, 0, owners, third)
    receive(1)
    receive(2)


def sum_kernel(plan, plane, plane3, tables, pick, win1, win2, lhs, out_ref, out, cells, plane1, plane2, *refs):
    bases1, bases2, sems = refs
    chunks, taps = plan.cols // CHUNK, plan.taps
    tiles = taps // CHUNK
    spread = Spread(plan)
    count1, count2 = plan.part_rows[1], plan.part_rows[2]
    number1, number2 = plan.part_cols[1] // CHUNK, plan.part_cols[2] // CHUNK

    def put(chunk):
        spot = slice(chunk * CHUNK, (chunk + 1) * CHUNK)
        return pltpu.make_async_copy(out.at[:, spot], out_ref.at[:, spot], sems.at[chunk])

    def fill(count, bases, sides):
        number = len(sides[0])
        shifts = Shifts(bases)
        return [
            taps_queue(
                lhs, shifts, (0, plan.rows), count, dict(enumerate(side)), tiles, (unit,), range(number + tiles - 1)
            )
            for unit, side in enumerate(sides)
        ]

    def keep(into, sides):
        count = into.shape[0]
        for chunk, (left, right) in enumerate(zip(*sides)):
            both = pltpu.matmul_pop(left) + pltpu.matmul_pop(right)
            into[:, chunk * CHUNK : (chunk + 1) * CHUNK] = power(both[:count], both[count:])

    half = chunks // 2

    def halves(accs, sizes):
        each = len(accs) // 2
        groups, at = [], 0
        for size in sizes:
            groups.append([accs[unit * each + at : unit * each + at + size] for unit in (0, 1)])
            at += size
        return groups

    def flat(sides):
        return [acc for side in sides for acc in side]

    for chunk in range(chunks):
        cells[chunk, spread.used :] = jnp.zeros((CHUNK - spread.used, CHUNK), cells.dtype)

    def parts(*accs):
        sides2, sides1, spreads = halves(accs, (number2, number1, half))
        fill_bases(win2, bases2, 0, (plan.part_cols[2] + taps) // LANES)
        fill_bases(win1, bases1, 0, (plan.part_cols[1] + taps) // LANES)
        queues = zip(
            spread.queues(3, plane3, tables, flat(spreads)),
            fill(count2, bases2, sides2),
            fill(count1, bases1, sides1),
        )
        drive([sum(queue, []) for queue in queues])
        spread.drain(3, flat(spreads), cells)
        keep(plane2, sides2)
        keep(plane1, sides1)

    pl.run_scoped(parts, *units([2 * count2] * number2 + [2 * count1] * number1 + [plan.part_rows[3]] * half))

    def total(*accs):
        spreads2, spreads1, sides = halves(accs, (half, half, half))
        totals = [sides[chunk % 2][chunk // 2] for chunk in range(chunks)]
        queues = zip(
            spread.queues(2, plane2, tables, flat(spreads2)),
            spread.queues(1, plane1, tables, flat(spreads1)),
        )
        drive([sum(queue, []) for queue in queues])
        spread.drain(2, flat(spreads2), cells)
        spread.drain(1, flat(spreads1), cells)
        drive(
            [
                [
                    (lambda chunk=chunk: cells[chunk], [(totals[chunk], lambda: pick[...])])
                    for chunk in range(unit, chunks, 2)
                ]
                for unit in (0, 1)
            ]
        )
        for chunk in range(chunks):
            spot = slice(chunk * CHUNK, (chunk + 1) * CHUNK)
            out[:, spot] = plane[:, spot].astype(jnp.float32) + pltpu.matmul_pop(totals[chunk])
            put(chunk).start()

    pl.run_scoped(total, *units([count2] * half + [count1] * half + [plan.rows] * half))
    for chunk in range(chunks):
        put(chunk).wait()


def body(spectrum, template_bank, template_index):
    owners = lax.axis_size("freq")
    taps = template_bank.shape[2]
    rows = template_index.shape[0]
    cols = spectrum.shape[1]
    plan = Plan(cols, taps, rows, owners)
    hbm = pl.BlockSpec(memory_space=pltpu.HBM)
    vmem = pl.BlockSpec(memory_space=pltpu.VMEM)
    wide = [width + taps for width in plan.part_cols]

    def held(*shape, kind=jnp.bfloat16):
        return pltpu.VMEM(shape, kind)

    between = (
        held(rows, cols),
        held(plan.part_rows[3], plan.part_cols[3]),
        held(len(Spread(plan).tables), CHUNK, CHUNK),
        held(rows, CHUNK),
        held(2, wide[1]),
        held(2, wide[2]),
        held(2 * taps // LANES, 2 * rows, LANES),
    )
    inputs = (spectrum, template_index.reshape(1, rows), template_bank)
    results = pl.pallas_call(
        functools.partial(planes_kernel, plan),
        out_shape=between,
        in_specs=[hbm] * 3,
        out_specs=(vmem,) * len(between),
        scratch_shapes=[
            held(2, wide[0]),
            held(2, wide[3]),
            *[held(2, wide[part] // LANES, TILE, LANES) for part in (0, 3)],
            held(taps // LANES, *template_bank.shape[:2], LANES),
            held(1, rows, kind=jnp.int32),
            held(2, plan.granule),
            held(2, max(plan.granule * plan.most, *wide)),
            pltpu.SemaphoreType.DMA((2 + taps // LANES,)),
            pltpu.SemaphoreType.DMA,
            pltpu.SemaphoreType.DMA((len(RATIOS),)),
            pltpu.SemaphoreType.REGULAR,
        ],
        compiler_params=pltpu.CompilerParams(collective_id=0, has_side_effects=True, vmem_limit_bytes=24 * 2**20),
        name="planes",
    )(*[pltpu.with_memory_space_constraint(x, pltpu.HBM) for x in inputs])
    return pl.pallas_call(
        functools.partial(sum_kernel, plan),
        out_shape=jax.ShapeDtypeStruct((rows, cols), jnp.float32),
        in_specs=[vmem] * len(between),
        out_specs=hbm,
        scratch_shapes=[
            held(rows, cols, kind=jnp.float32),
            held(cols // CHUNK, CHUNK, CHUNK),
            *[held(plan.part_rows[part], plan.part_cols[part]) for part in (1, 2)],
            *[held(2, wide[part] // LANES, TILE, LANES) for part in (1, 2)],
            pltpu.SemaphoreType.DMA((cols // CHUNK,)),
        ],
        compiler_params=pltpu.CompilerParams(vmem_limit_bytes=24 * 2**20),
        name="sums",
    )(*results)


def solution(mesh):
    return jax.shard_map(
        body,
        mesh=mesh,
        in_specs=(P(None, ("beam", "freq")), P(), P()),
        out_specs=P(None, ("beam", "freq")),
        check_vma=False,
    )
```

```python
import functools

import jax
import jax.numpy as jnp
from jax import lax
from jax.experimental import pallas as pl
from jax.experimental.pallas import tpu as pltpu
from jax.sharding import PartitionSpec as P

RATIOS = ((1, 1), (1, 2), (1, 4), (3, 4))
CHUNK = 256
LANES = 128
TILE = 16


class Plan:
    def __init__(self, cols, taps, rows, owners):
        self.cols, self.taps, self.rows, self.owners = cols, taps, rows, owners
        self.granule = taps // 2
        self.held = cols // self.granule
        self.steps = [self.held * n // d for n, d in RATIOS]
        self.part_cols = [cols * n // d for n, d in RATIOS]
        self.part_rows = [rows * n // d for n, d in RATIOS]
        self.most = max(sum(count for _, _, _, count, _ in self.sends(source)) for source in range(owners))

    def pieces(self, source, target):
        found = []
        for part, step in enumerate(self.steps):
            first = step * target - 1
            low = max(self.held * source, first)
            high = min(self.held * (source + 1), first + step + 2)
            if low < high and (part or source != target):
                found.append((part, target, low - self.held * source, high - low, low - first))
        return found

    def sends(self, source):
        near = range(max(0, source - 1), min(self.owners, 4 * source + 8))
        return [piece for target in near for piece in self.pieces(source, target)]

    def far(self, source, target):
        return not any(part in (0, len(RATIOS) - 1) for part, *_ in self.pieces(source, target))

    def targets(self, me, far):
        return [to for to in range(self.owners) if to != me and self.far(me, to) == far and self.pieces(me, to)]

    def sources(self, me, far):
        return [by for by in range(self.owners) if by != me and self.far(by, me) == far and self.pieces(by, me)]


def choose(me, low, high, act):
    if high - low == 1:
        act(low)
    else:
        middle = (low + high) // 2
        pl.when(me < middle)(lambda: choose(me, low, middle, act))
        pl.when(me >= middle)(lambda: choose(me, middle, high, act))


def one_hot(shape, make):
    left = lax.broadcasted_iota(jnp.int32, shape, 0)
    right = lax.broadcasted_iota(jnp.int32, shape, 1)
    return make(left, right).astype(jnp.float32).astype(jnp.bfloat16)


def fill_bases(window, bases, low, high, spare=0):
    width = (high - low) * LANES
    for which in (0, 1):
        line = window[which : which + 1, low * LANES : high * LANES].astype(jnp.float32)
        base = jnp.broadcast_to(line, (8, width))
        place = lax.broadcasted_iota(jnp.int32, (8, width), 0)
        for bit in (1, 2, 4):
            base = jnp.where((place & bit) != 0, pltpu.roll(base, width - bit, 1), base)
        base = jnp.concatenate([base, pltpu.roll(base, width - 8, 1)], 0).astype(jnp.bfloat16)
        for block in range(low, high - spare):
            bases[which, block] = base[:, (block - low) * LANES : (block - low + 1) * LANES]


class Shifts:
    def __init__(self, bases):
        self.bases = bases
        self.turned, self.blocks = {}, {}
        lane = lax.broadcasted_iota(jnp.int32, (TILE, LANES), 1)
        self.keep = [lane < LANES - TILE * turn for turn in range(LANES // TILE)]

    def turn(self, which, block, turn):
        key = which, block, turn
        if key not in self.turned:
            value = self.bases[which, block]
            self.turned[key] = pltpu.roll(value, LANES - TILE * turn, 1) if turn else value
        return self.turned[key]

    def block(self, which, block):
        key = which, block
        if key not in self.blocks:
            rows = [self.turn(which, block, 0)]
            for turn in range(1, LANES // TILE):
                rows.append(
                    jnp.where(self.keep[turn], self.turn(which, block, turn), self.turn(which, block + 1, turn))
                )
            self.blocks[key] = jnp.concatenate(rows, 0)
        return self.blocks[key]

    def tile(self, which, spot):
        each = CHUNK // LANES
        return jnp.concatenate(
            [
                jnp.concatenate([self.block(which, each * spot + at + row) for row in range(each)], 0)
                for at in range(each)
            ],
            1,
        )


def run(tasks):
    for task in tasks:
        task()


def rows_of(lhs, first, count, which, tile):
    half = lhs.shape[0] // 2
    each = CHUNK // LANES
    slabs = [which * half + each * tile + at for at in range(each)]
    return jnp.concatenate(
        [jnp.concatenate([lhs[slab, row : row + count] for row in first], 0) for slab in slabs], 1
    )


def drive(queues):
    longest = max(len(queue) for queue in queues)
    for step in range(longest + 1):
        for unit, queue in enumerate(queues):
            if step < len(queue):
                pltpu.matmul_push_rhs(queue[step][0](), staging_register=step % 2, mxu_index=unit)
        for unit, queue in enumerate(queues):
            if 0 < step <= len(queue):
                for number, (acc, rows) in enumerate(queue[step - 1][1]):
                    pltpu.matmul_acc_lhs(acc, rows(), load_staged_rhs=None if number else (step - 1) % 2)


def taps_queue(lhs, shifts, first, count, accs, tiles, kinds, spots):
    return [
        (
            functools.partial(shifts.tile, which, spot),
            [
                (acc, functools.partial(rows_of, lhs, first, count, which, spot - chunk))
                for chunk, acc in accs.items()
                if 0 <= spot - chunk < tiles
            ],
        )
        for which in kinds
        for spot in spots
    ]


def power(real, imag):
    return (real * real + imag * imag).astype(jnp.bfloat16)


def units(shapes):
    return [pltpu.ACC(unit)((rows, CHUNK), jnp.float32) for unit in (0, 1) for rows in shapes]


class Spread:
    def __init__(self, plan):
        self.plan = plan
        self.chunks = plan.cols // CHUNK
        self.belows = [sum(plan.part_rows[1:part]) for part in range(len(RATIOS))]
        self.used = sum(plan.part_rows[1:])
        self.tables = sorted(
            {(part, self.place(part, chunk)[1]) for part in range(1, len(RATIOS)) for chunk in range(self.chunks)}
        )

    def place(self, part, chunk):
        start = CHUNK * RATIOS[part][0] // RATIOS[part][1] * chunk
        base = min(start // LANES * LANES, self.plan.part_cols[part] - CHUNK)
        return base, start - base

    def prepare(self, tables, pick):
        for number, (part, skip) in enumerate(self.tables):
            n, d = RATIOS[part]
            tables[number] = one_hot((CHUNK, CHUNK), lambda k, r: k == skip + r * n // d)
        left = lax.broadcasted_iota(jnp.int32, pick.shape, 0)
        right = lax.broadcasted_iota(jnp.int32, pick.shape, 1)
        hits = [right == self.belows[part] + left * n // d for part, (n, d) in enumerate(RATIOS) if part]
        pick[...] = functools.reduce(jnp.logical_or, hits).astype(jnp.float32).astype(jnp.bfloat16)

    def queues(self, part, plane, tables, accs):
        half = self.chunks // 2
        found = []
        for unit in (0, 1):
            mine = list(range(unit, self.chunks, 2))
            queue = []
            for skip in sorted({self.place(part, chunk)[1] for chunk in mine}):
                number = self.tables.index((part, skip))
                users = []
                for chunk in mine:
                    base, skipped = self.place(part, chunk)
                    if skipped == skip:
                        users.append((accs[unit * half + chunk // 2], lambda base=base: plane[:, base : base + CHUNK]))
                queue.append((lambda number=number: tables[number], users))
            found.append(queue)
        return found

    def drain(self, part, accs, cells):
        count, below = self.plan.part_rows[part], self.belows[part]
        for chunk in range(self.chunks):
            acc = accs[chunk % 2 * (self.chunks // 2) + chunk // 2]
            cells[chunk, below : below + count] = pltpu.matmul_pop(acc).astype(jnp.bfloat16)


def planes_kernel(plan, spec_ref, index_ref, bank_ref, plane, plane3, tables, pick, win1, win2, lhs, win, win3, *refs):
    bases, bases3, bank, index, zeros, sized, in_sems, send_sem, recv_sems, ready = refs
    wins = (win, win1, win2, win3)
    rows, taps, size, cols, owners = plan.rows, plan.taps, plan.granule, plan.cols, plan.owners
    parts = len(RATIOS)
    me = lax.axis_index("freq")

    fetch_own = pltpu.make_async_copy(spec_ref, win.at[:, size : size + cols], in_sems.at[0])
    fetch_own.start()
    barrier = pltpu.get_barrier_semaphore()

    def signal(semaphore, peer):
        pl.semaphore_signal(semaphore, inc=1, device_id={"freq": peer}, device_id_type=pl.DeviceIdType.MESH)

    def greet(k):
        for peer in plan.sources(k, False) + plan.targets(k, True):
            signal(barrier, peer)

    choose(me, 0, owners, greet)
    fetch_index = pltpu.make_async_copy(index_ref, index, in_sems.at[1])
    fetch_index.start()
    fetch_bank = [
        pltpu.make_async_copy(bank_ref.at[:, :, slab * LANES : (slab + 1) * LANES], bank.at[slab], in_sems.at[2 + slab])
        for slab in range(taps // LANES)
    ]
    run([fetch.start for fetch in fetch_bank])
    zeros[...] = jnp.zeros(zeros.shape, zeros.dtype)

    def send(k, far):
        for part, to, begin, count, place in reversed(plan.sends(k)):
            source = win.at[:, size * (1 + begin) : size * (1 + begin + count)]
            target = wins[part].at[:, size * place : size * (place + count)]
            if to == k:
                if not far:
                    pltpu.make_async_copy(source, target, recv_sems.at[part]).start()
            elif plan.far(k, to) == far:
                pltpu.make_async_remote_copy(
                    src_ref=source,
                    dst_ref=target,
                    send_sem=send_sem,
                    recv_sem=recv_sems.at[part],
                    device_id={"freq": to},
                    device_id_type=pl.DeviceIdType.MESH,
                ).start()

    def fill(part, spot):
        pltpu.make_async_copy(zeros, wins[part].at[:, spot : spot + size], recv_sems.at[part]).start()

    def first(k):
        count = len(plan.targets(k, False)) + len(plan.sources(k, True))
        if count:
            pl.semaphore_wait(barrier, count)
        for peer in plan.sources(k, True):
            signal(ready, peer)
        send(k, False)
        if k == 0:
            for part in range(parts):
                fill(part, 0)
        if k == owners - 1:
            fill(0, size + cols)

    def second(k, early):
        if early != (k >= owners // 8):
            return
        count = len(plan.targets(k, True))
        if count:
            pl.semaphore_wait(ready, count)
            send(k, True)

    def third(k):
        total = sum(count for _, to, _, count, _ in plan.sends(k) if to != k)
        if total:
            whole = sized.at[:, : total * size]
            pltpu.make_async_copy(whole, whole, send_sem).wait()

    def receive(part):
        whole = sized.at[:, : 2 * size if part == 0 else plan.part_cols[part] + taps]
        pltpu.make_async_copy(whole, whole, recv_sems.at[part]).wait()

    blocks = (cols + taps) // LANES
    halo = size // LANES
    chunks = cols // CHUNK
    tiles = taps // CHUNK
    low, high = size // CHUNK, (size + cols) // CHUNK - 1

    spread = Spread(plan)
    spread.prepare(tables, pick)
    fetch_index.wait()
    names = lax.broadcasted_iota(jnp.int32, (bank.shape[2], rows), 0)
    picks = (names == index[...]).astype(jnp.float32).T.astype(jnp.bfloat16)
    fetch_own.wait()
    fill_bases(win, bases, halo, blocks - halo)
    choose(me, 0, owners, first)
    run([fetch.wait for fetch in fetch_bank])

    def gather(*accs):
        drive(
            [
                [
                    (
                        lambda deep=deep, wide=wide, unit=unit: jnp.concatenate(
                            [
                                bank[wide * CHUNK // LANES + at, unit, deep * CHUNK : (deep + 1) * CHUNK]
                                for at in range(CHUNK // LANES)
                            ],
                            1,
                        ),
                        [(accs[unit * tiles + wide], lambda deep=deep: picks[:, deep * CHUNK : (deep + 1) * CHUNK])],
                    )
                    for wide in range(tiles)
                    for deep in range(bank.shape[2] // CHUNK)
                ]
                for unit in (0, 1)
            ],
        )
        slabs = taps // LANES
        for tile in range(tiles):
            real = pltpu.matmul_pop(accs[tile]).astype(jnp.bfloat16)
            imag = pltpu.matmul_pop(accs[tiles + tile]).astype(jnp.bfloat16)
            for at in range(0, CHUNK, LANES):
                slab, piece = (tile * CHUNK + at) // LANES, slice(at, at + LANES)
                lhs[slab, :rows] = real[:, piece]
                lhs[slab, rows:] = imag[:, piece]
                lhs[slabs + slab, :rows] = -imag[:, piece]
                lhs[slabs + slab, rows:] = real[:, piece]

    pl.run_scoped(gather, *units([rows] * tiles))
    inner = [chunk for chunk in range(chunks) if low <= chunk and chunk + tiles <= high]

    def split(sides, base, count, chosen):
        return [
            taps_queue(lhs, Shifts(base), (0, rows), count, side, tiles, (0, 1), [spot for spot in spots if chosen(spot)])
            for side in sides
            for spots in [range(min(side), max(side) + tiles)]
        ]

    def sided(accs, number):
        each = len(accs) // 2
        sides = []
        for unit in (0, 1):
            mine = range(unit * number // 2, (unit + 1) * number // 2)
            if number == chunks:
                mine = sorted(mine, key=lambda chunk: chunk in inner)
            sides.append(dict(zip(mine, accs[unit * each + each - len(mine) : (unit + 1) * each])))
        return sides

    def keep(into, sides, chosen):
        count = into.shape[0]
        for side in sides:
            for chunk in sorted(side):
                if chunk in chosen:
                    both = pltpu.matmul_pop(side[chunk])
                    into[:, chunk * CHUNK : (chunk + 1) * CHUNK] = power(both[:count], both[count:])

    def part0(*accs):
        sides = sided(accs, chunks)
        drive(split(sides, bases, rows, lambda spot: low <= spot < high))
        choose(me, 0, owners, functools.partial(second, early=True))
        keep(plane, sides, inner)
        receive(0)
        receive(3)
        fill_bases(win, bases, 0, halo + 1, 1)
        fill_bases(win, bases, blocks - halo - 1, blocks)
        drive(split(sides, bases, rows, lambda spot: not low <= spot < high))
        fill_bases(win3, bases3, 0, (plan.part_cols[3] + taps) // LANES)
        keep(plane, sides, [chunk for chunk in range(chunks) if chunk not in inner])

    pl.run_scoped(part0, *units([2 * rows] * (chunks // 2)))
    choose(me, 0, owners, functools.partial(second, early=False))
    count3 = plan.part_rows[3]
    number3 = plan.part_cols[3] // CHUNK

    def part3(*accs):
        sides = sided(accs, number3)
        drive(split(sides, bases3, count3, lambda spot: True))
        keep(plane3, sides, range(number3))

    pl.run_scoped(part3, *units([2 * count3] * (number3 // 2)))

    choose(me, 0, owners, third)
    receive(1)
    receive(2)


def sum_kernel(plan, plane, plane3, tables, pick, win1, win2, lhs, out_ref, out, cells, plane1, plane2, *refs):
    bases1, bases2, sems = refs
    chunks, taps = plan.cols // CHUNK, plan.taps
    tiles = taps // CHUNK
    spread = Spread(plan)
    count1, count2 = plan.part_rows[1], plan.part_rows[2]
    number1, number2 = plan.part_cols[1] // CHUNK, plan.part_cols[2] // CHUNK

    def put(chunk):
        spot = slice(chunk * CHUNK, (chunk + 1) * CHUNK)
        return pltpu.make_async_copy(out.at[:, spot], out_ref.at[:, spot], sems.at[chunk])

    def fill(count, bases, sides):
        number = len(sides[0])
        shifts = Shifts(bases)
        return [
            taps_queue(
                lhs, shifts, (0, plan.rows), count, dict(enumerate(side)), tiles, (unit,), range(number + tiles - 1)
            )
            for unit, side in enumerate(sides)
        ]

    def keep(into, sides):
        count = into.shape[0]
        for chunk, (left, right) in enumerate(zip(*sides)):
            both = pltpu.matmul_pop(left) + pltpu.matmul_pop(right)
            into[:, chunk * CHUNK : (chunk + 1) * CHUNK] = power(both[:count], both[count:])

    half = chunks // 2

    def halves(accs, sizes):
        each = len(accs) // 2
        groups, at = [], 0
        for size in sizes:
            groups.append([accs[unit * each + at : unit * each + at + size] for unit in (0, 1)])
            at += size
        return groups

    def flat(sides):
        return [acc for side in sides for acc in side]

    for chunk in range(chunks):
        cells[chunk, spread.used :] = jnp.zeros((CHUNK - spread.used, CHUNK), cells.dtype)

    def parts(*accs):
        sides2, sides1, spreads = halves(accs, (number2, number1, half))
        fill_bases(win2, bases2, 0, (plan.part_cols[2] + taps) // LANES)
        fill_bases(win1, bases1, 0, (plan.part_cols[1] + taps) // LANES)
        queues = zip(
            spread.queues(3, plane3, tables, flat(spreads)),
            fill(count2, bases2, sides2),
            fill(count1, bases1, sides1),
        )
        drive([sum(queue, []) for queue in queues])
        spread.drain(3, flat(spreads), cells)
        keep(plane2, sides2)
        keep(plane1, sides1)

    pl.run_scoped(parts, *units([2 * count2] * number2 + [2 * count1] * number1 + [plan.part_rows[3]] * half))

    def total(*accs):
        spreads2, spreads1, sides = halves(accs, (half, half, half))
        totals = [sides[chunk % 2][chunk // 2] for chunk in range(chunks)]
        queues = zip(
            spread.queues(2, plane2, tables, flat(spreads2)),
            spread.queues(1, plane1, tables, flat(spreads1)),
        )
        drive([sum(queue, []) for queue in queues])
        spread.drain(2, flat(spreads2), cells)
        spread.drain(1, flat(spreads1), cells)
        drive(
            [
                [
                    (lambda chunk=chunk: cells[chunk], [(totals[chunk], lambda: pick[...])])
                    for chunk in range(unit, chunks, 2)
                ]
                for unit in (0, 1)
            ]
        )
        for chunk in range(chunks):
            spot = slice(chunk * CHUNK, (chunk + 1) * CHUNK)
            out[:, spot] = plane[:, spot].astype(jnp.float32) + pltpu.matmul_pop(totals[chunk])
            put(chunk).start()

    pl.run_scoped(total, *units([count2] * half + [count1] * half + [plan.rows] * half))
    for chunk in range(chunks):
        put(chunk).wait()


def body(spectrum, template_bank, template_index):
    owners = lax.axis_size("freq")
    taps = template_bank.shape[2]
    rows = template_index.shape[0]
    cols = spectrum.shape[1]
    plan = Plan(cols, taps, rows, owners)
    hbm = pl.BlockSpec(memory_space=pltpu.HBM)
    vmem = pl.BlockSpec(memory_space=pltpu.VMEM)
    wide = [width + taps for width in plan.part_cols]

    def held(*shape, kind=jnp.bfloat16):
        return pltpu.VMEM(shape, kind)

    between = (
        held(rows, cols),
        held(plan.part_rows[3], plan.part_cols[3]),
        held(len(Spread(plan).tables), CHUNK, CHUNK),
        held(rows, CHUNK),
        held(2, wide[1]),
        held(2, wide[2]),
        held(2 * taps // LANES, 2 * rows, LANES),
    )
    inputs = (spectrum, template_index.reshape(1, rows), template_bank)
    results = pl.pallas_call(
        functools.partial(planes_kernel, plan),
        out_shape=between,
        in_specs=[hbm] * 3,
        out_specs=(vmem,) * len(between),
        scratch_shapes=[
            held(2, wide[0]),
            held(2, wide[3]),
            *[held(2, wide[part] // LANES, TILE, LANES) for part in (0, 3)],
            held(taps // LANES, *template_bank.shape[:2], LANES),
            held(1, rows, kind=jnp.int32),
            held(2, plan.granule),
            held(2, max(plan.granule * plan.most, *wide)),
            pltpu.SemaphoreType.DMA((2 + taps // LANES,)),
            pltpu.SemaphoreType.DMA,
            pltpu.SemaphoreType.DMA((len(RATIOS),)),
            pltpu.SemaphoreType.REGULAR,
        ],
        compiler_params=pltpu.CompilerParams(collective_id=0, has_side_effects=True, vmem_limit_bytes=24 * 2**20),
        name="planes",
    )(*[pltpu.with_memory_space_constraint(x, pltpu.HBM) for x in inputs])
    return pl.pallas_call(
        functools.partial(sum_kernel, plan),
        out_shape=jax.ShapeDtypeStruct((rows, cols), jnp.float32),
        in_specs=[vmem] * len(between),
        out_specs=hbm,
        scratch_shapes=[
            held(rows, cols, kind=jnp.float32),
            held(cols // CHUNK, CHUNK, CHUNK),
            *[held(plan.part_rows[part], plan.part_cols[part]) for part in (1, 2)],
            *[held(2, wide[part] // LANES, TILE, LANES) for part in (1, 2)],
            pltpu.SemaphoreType.DMA((cols // CHUNK,)),
        ],
        compiler_params=pltpu.CompilerParams(vmem_limit_bytes=24 * 2**20),
        name="sums",
    )(*results)


def solution(mesh):
    return jax.shard_map(
        body,
        mesh=mesh,
        in_specs=(P(None, ("beam", "freq")), P(), P()),
        out_specs=P(None, ("beam", "freq")),
        check_vma=False,
    )
```

```python
import functools

import jax
import jax.numpy as jnp
from jax import lax
from jax.experimental import pallas as pl
from jax.experimental.pallas import tpu as pltpu
from jax.sharding import PartitionSpec as P

RATIOS = ((1, 1), (1, 2), (1, 4), (3, 4))
CHUNK = 256
LANES = 128
TILE = 16


class Plan:
    def __init__(self, cols, taps, rows, owners):
        self.cols, self.taps, self.rows, self.owners = cols, taps, rows, owners
        self.granule = taps // 2
        self.held = cols // self.granule
        self.steps = [self.held * n // d for n, d in RATIOS]
        self.part_cols = [cols * n // d for n, d in RATIOS]
        self.part_rows = [rows * n // d for n, d in RATIOS]
        self.most = max(sum(count for _, _, _, count, _ in self.sends(source)) for source in range(owners))

    def pieces(self, source, target):
        found = []
        for part, step in enumerate(self.steps):
            first = step * target - 1
            low = max(self.held * source, first)
            high = min(self.held * (source + 1), first + step + 2)
            if low < high and (part or source != target):
                found.append((part, target, low - self.held * source, high - low, low - first))
        return found

    def sends(self, source):
        near = range(max(0, source - 1), min(self.owners, 4 * source + 8))
        return [piece for target in near for piece in self.pieces(source, target)]

    def far(self, source, target):
        return not any(part in (0, len(RATIOS) - 1) for part, *_ in self.pieces(source, target))

    def targets(self, me, far):
        return [to for to in range(self.owners) if to != me and self.far(me, to) == far and self.pieces(me, to)]

    def sources(self, me, far):
        return [by for by in range(self.owners) if by != me and self.far(by, me) == far and self.pieces(by, me)]


def choose(me, low, high, act):
    if high - low == 1:
        act(low)
    else:
        middle = (low + high) // 2
        pl.when(me < middle)(lambda: choose(me, low, middle, act))
        pl.when(me >= middle)(lambda: choose(me, middle, high, act))


def one_hot(shape, make):
    left = lax.broadcasted_iota(jnp.int32, shape, 0)
    right = lax.broadcasted_iota(jnp.int32, shape, 1)
    return make(left, right).astype(jnp.float32).astype(jnp.bfloat16)


def fill_bases(window, bases, low, high, spare=0):
    width = (high - low) * LANES
    for which in (0, 1):
        line = window[which : which + 1, low * LANES : high * LANES].astype(jnp.float32)
        base = jnp.broadcast_to(line, (8, width))
        place = lax.broadcasted_iota(jnp.int32, (8, width), 0)
        for bit in (1, 2, 4):
            base = jnp.where((place & bit) != 0, pltpu.roll(base, width - bit, 1), base)
        base = jnp.concatenate([base, pltpu.roll(base, width - 8, 1)], 0).astype(jnp.bfloat16)
        for block in range(low, high - spare):
            bases[which, block] = base[:, (block - low) * LANES : (block - low + 1) * LANES]


class Shifts:
    def __init__(self, bases):
        self.bases = bases
        self.turned, self.blocks = {}, {}
        lane = lax.broadcasted_iota(jnp.int32, (TILE, LANES), 1)
        self.keep = [lane < LANES - TILE * turn for turn in range(LANES // TILE)]

    def turn(self, which, block, turn):
        key = which, block, turn
        if key not in self.turned:
            value = self.bases[which, block]
            self.turned[key] = pltpu.roll(value, LANES - TILE * turn, 1) if turn else value
        return self.turned[key]

    def block(self, which, block):
        key = which, block
        if key not in self.blocks:
            rows = [self.turn(which, block, 0)]
            for turn in range(1, LANES // TILE):
                rows.append(
                    jnp.where(self.keep[turn], self.turn(which, block, turn), self.turn(which, block + 1, turn))
                )
            self.blocks[key] = jnp.concatenate(rows, 0)
        return self.blocks[key]

    def tile(self, which, spot):
        each = CHUNK // LANES
        return jnp.concatenate(
            [
                jnp.concatenate([self.block(which, each * spot + at + row) for row in range(each)], 0)
                for at in range(each)
            ],
            1,
        )


def run(tasks):
    for task in tasks:
        task()


def rows_of(lhs, first, count, which, tile):
    half = lhs.shape[0] // 2
    each = CHUNK // LANES
    slabs = [which * half + each * tile + at for at in range(each)]
    return jnp.concatenate(
        [jnp.concatenate([lhs[slab, row : row + count] for row in first], 0) for slab in slabs], 1
    )


def drive(queues):
    longest = max(len(queue) for queue in queues)
    for step in range(longest + 1):
        for unit, queue in enumerate(queues):
            if step < len(queue):
                pltpu.matmul_push_rhs(queue[step][0](), staging_register=step % 2, mxu_index=unit)
        for unit, queue in enumerate(queues):
            if 0 < step <= len(queue):
                for number, (acc, rows) in enumerate(queue[step - 1][1]):
                    pltpu.matmul_acc_lhs(acc, rows(), load_staged_rhs=None if number else (step - 1) % 2)


def taps_queue(lhs, shifts, first, count, accs, tiles, kinds, spots):
    return [
        (
            functools.partial(shifts.tile, which, spot),
            [
                (acc, functools.partial(rows_of, lhs, first, count, which, spot - chunk))
                for chunk, acc in accs.items()
                if 0 <= spot - chunk < tiles
            ],
        )
        for which in kinds
        for spot in spots
    ]


def power(real, imag):
    return (real * real + imag * imag).astype(jnp.bfloat16)


def units(shapes):
    return [pltpu.ACC(unit)((rows, CHUNK), jnp.float32) for unit in (0, 1) for rows in shapes]


class Spread:
    def __init__(self, plan):
        self.plan = plan
        self.chunks = plan.cols // CHUNK
        self.belows = [sum(plan.part_rows[1:part]) for part in range(len(RATIOS))]
        self.used = sum(plan.part_rows[1:])
        self.tables = sorted(
            {(part, self.place(part, chunk)[1]) for part in range(1, len(RATIOS)) for chunk in range(self.chunks)}
        )

    def place(self, part, chunk):
        start = CHUNK * RATIOS[part][0] // RATIOS[part][1] * chunk
        base = min(start // LANES * LANES, self.plan.part_cols[part] - CHUNK)
        return base, start - base

    def prepare(self, tables, pick):
        for number, (part, skip) in enumerate(self.tables):
            n, d = RATIOS[part]
            tables[number] = one_hot((CHUNK, CHUNK), lambda k, r: k == skip + r * n // d)
        left = lax.broadcasted_iota(jnp.int32, pick.shape, 0)
        right = lax.broadcasted_iota(jnp.int32, pick.shape, 1)
        hits = [right == self.belows[part] + left * n // d for part, (n, d) in enumerate(RATIOS) if part]
        pick[...] = functools.reduce(jnp.logical_or, hits).astype(jnp.float32).astype(jnp.bfloat16)

    def queues(self, part, plane, tables, accs):
        half = self.chunks // 2
        found = []
        for unit in (0, 1):
            mine = list(range(unit, self.chunks, 2))
            queue = []
            for skip in sorted({self.place(part, chunk)[1] for chunk in mine}):
                number = self.tables.index((part, skip))
                users = []
                for chunk in mine:
                    base, skipped = self.place(part, chunk)
                    if skipped == skip:
                        users.append((accs[unit * half + chunk // 2], lambda base=base: plane[:, base : base + CHUNK]))
                queue.append((lambda number=number: tables[number], users))
            found.append(queue)
        return found

    def drain(self, part, accs, cells):
        count, below = self.plan.part_rows[part], self.belows[part]
        for chunk in range(self.chunks):
            acc = accs[chunk % 2 * (self.chunks // 2) + chunk // 2]
            cells[chunk, below : below + count] = pltpu.matmul_pop(acc).astype(jnp.bfloat16)


def planes_kernel(plan, spec_ref, index_ref, bank_ref, plane, plane3, tables, pick, win1, win2, lhs, win, win3, *refs):
    bases, bases3, bank, index, zeros, sized, in_sems, send_sem, recv_sems, ready = refs
    wins = (win, win1, win2, win3)
    rows, taps, size, cols, owners = plan.rows, plan.taps, plan.granule, plan.cols, plan.owners
    parts = len(RATIOS)
    me = lax.axis_index("freq")

    fetch_own = pltpu.make_async_copy(spec_ref, win.at[:, size : size + cols], in_sems.at[0])
    fetch_own.start()
    barrier = pltpu.get_barrier_semaphore()

    def signal(semaphore, peer):
        pl.semaphore_signal(semaphore, inc=1, device_id={"freq": peer}, device_id_type=pl.DeviceIdType.MESH)

    def greet(k):
        for peer in plan.sources(k, False) + plan.targets(k, True):
            signal(barrier, peer)

    choose(me, 0, owners, greet)
    fetch_index = pltpu.make_async_copy(index_ref, index, in_sems.at[1])
    fetch_index.start()
    fetch_bank = [
        pltpu.make_async_copy(bank_ref.at[:, :, slab * LANES : (slab + 1) * LANES], bank.at[slab], in_sems.at[2 + slab])
        for slab in range(taps // LANES)
    ]
    run([fetch.start for fetch in fetch_bank])
    zeros[...] = jnp.zeros(zeros.shape, zeros.dtype)

    def send(k, far):
        for part, to, begin, count, place in sorted(plan.sends(k), key=lambda piece: (piece[0] % (len(RATIOS) - 1) > 0, -piece[1])):
            source = win.at[:, size * (1 + begin) : size * (1 + begin + count)]
            target = wins[part].at[:, size * place : size * (place + count)]
            if to == k:
                if not far:
                    pltpu.make_async_copy(source, target, recv_sems.at[part]).start()
            elif plan.far(k, to) == far:
                pltpu.make_async_remote_copy(
                    src_ref=source,
                    dst_ref=target,
                    send_sem=send_sem,
                    recv_sem=recv_sems.at[part],
                    device_id={"freq": to},
                    device_id_type=pl.DeviceIdType.MESH,
                ).start()

    def fill(part, spot):
        pltpu.make_async_copy(zeros, wins[part].at[:, spot : spot + size], recv_sems.at[part]).start()

    def first(k):
        count = len(plan.targets(k, False)) + len(plan.sources(k, True))
        if count:
            pl.semaphore_wait(barrier, count)
        for peer in plan.sources(k, True):
            signal(ready, peer)
        send(k, False)
        if k == 0:
            for part in range(parts):
                fill(part, 0)
        if k == owners - 1:
            fill(0, size + cols)

    def second(k, early):
        if early != (k >= owners // 8):
            return
        count = len(plan.targets(k, True))
        if count:
            pl.semaphore_wait(ready, count)
            send(k, True)

    def third(k):
        total = sum(count for _, to, _, count, _ in plan.sends(k) if to != k)
        if total:
            whole = sized.at[:, : total * size]
            pltpu.make_async_copy(whole, whole, send_sem).wait()

    def receive(part):
        whole = sized.at[:, : 2 * size if part == 0 else plan.part_cols[part] + taps]
        pltpu.make_async_copy(whole, whole, recv_sems.at[part]).wait()

    blocks = (cols + taps) // LANES
    halo = size // LANES
    chunks = cols // CHUNK
    tiles = taps // CHUNK
    low, high = size // CHUNK, (size + cols) // CHUNK - 1

    spread = Spread(plan)
    spread.prepare(tables, pick)
    fetch_index.wait()
    names = lax.broadcasted_iota(jnp.int32, (bank.shape[2], rows), 0)
    picks = (names == index[...]).astype(jnp.float32).T.astype(jnp.bfloat16)
    fetch_own.wait()
    fill_bases(win, bases, halo, blocks - halo)
    choose(me, 0, owners, first)
    run([fetch.wait for fetch in fetch_bank])

    def gather(*accs):
        drive(
            [
                [
                    (
                        lambda deep=deep, wide=wide, unit=unit: jnp.concatenate(
                            [
                                bank[wide * CHUNK // LANES + at, unit, deep * CHUNK : (deep + 1) * CHUNK]
                                for at in range(CHUNK // LANES)
                            ],
                            1,
                        ),
                        [(accs[unit * tiles + wide], lambda deep=deep: picks[:, deep * CHUNK : (deep + 1) * CHUNK])],
                    )
                    for wide in range(tiles)
                    for deep in range(bank.shape[2] // CHUNK)
                ]
                for unit in (0, 1)
            ],
        )
        slabs = taps // LANES
        for tile in range(tiles):
            real = pltpu.matmul_pop(accs[tile]).astype(jnp.bfloat16)
            imag = pltpu.matmul_pop(accs[tiles + tile]).astype(jnp.bfloat16)
            for at in range(0, CHUNK, LANES):
                slab, piece = (tile * CHUNK + at) // LANES, slice(at, at + LANES)
                lhs[slab, :rows] = real[:, piece]
                lhs[slab, rows:] = imag[:, piece]
                lhs[slabs + slab, :rows] = -imag[:, piece]
                lhs[slabs + slab, rows:] = real[:, piece]

    pl.run_scoped(gather, *units([rows] * tiles))
    inner = [chunk for chunk in range(chunks) if low <= chunk and chunk + tiles <= high]

    def split(sides, base, count, chosen):
        return [
            taps_queue(lhs, Shifts(base), (0, rows), count, side, tiles, (0, 1), [spot for spot in spots if chosen(spot)])
            for side in sides
            for spots in [range(min(side), max(side) + tiles)]
        ]

    def sided(accs, number):
        each = len(accs) // 2
        sides = []
        for unit in (0, 1):
            mine = range(unit * number // 2, (unit + 1) * number // 2)
            if number == chunks:
                mine = sorted(mine, key=lambda chunk: chunk in inner)
            sides.append(dict(zip(mine, accs[unit * each + each - len(mine) : (unit + 1) * each])))
        return sides

    def keep(into, sides, chosen):
        count = into.shape[0]
        for side in sides:
            for chunk in sorted(side):
                if chunk in chosen:
                    both = pltpu.matmul_pop(side[chunk])
                    into[:, chunk * CHUNK : (chunk + 1) * CHUNK] = power(both[:count], both[count:])

    def part0(*accs):
        sides = sided(accs, chunks)
        drive(split(sides, bases, rows, lambda spot: low <= spot < high))
        choose(me, 0, owners, functools.partial(second, early=True))
        keep(plane, sides, inner)
        receive(0)
        receive(3)
        fill_bases(win, bases, 0, halo + 1, 1)
        fill_bases(win, bases, blocks - halo - 1, blocks)
        drive(split(sides, bases, rows, lambda spot: not low <= spot < high))
        fill_bases(win3, bases3, 0, (plan.part_cols[3] + taps) // LANES)
        keep(plane, sides, [chunk for chunk in range(chunks) if chunk not in inner])

    pl.run_scoped(part0, *units([2 * rows] * (chunks // 2)))
    choose(me, 0, owners, functools.partial(second, early=False))
    count3 = plan.part_rows[3]
    number3 = plan.part_cols[3] // CHUNK

    def part3(*accs):
        sides = sided(accs, number3)
        drive(split(sides, bases3, count3, lambda spot: True))
        keep(plane3, sides, range(number3))

    pl.run_scoped(part3, *units([2 * count3] * (number3 // 2)))

    choose(me, 0, owners, third)
    receive(1)
    receive(2)


def sum_kernel(plan, plane, plane3, tables, pick, win1, win2, lhs, out_ref, out, cells, plane1, plane2, *refs):
    bases1, bases2, sems = refs
    chunks, taps = plan.cols // CHUNK, plan.taps
    tiles = taps // CHUNK
    spread = Spread(plan)
    count1, count2 = plan.part_rows[1], plan.part_rows[2]
    number1, number2 = plan.part_cols[1] // CHUNK, plan.part_cols[2] // CHUNK

    def put(chunk):
        spot = slice(chunk * CHUNK, (chunk + 1) * CHUNK)
        return pltpu.make_async_copy(out.at[:, spot], out_ref.at[:, spot], sems.at[chunk])

    def fill(count, bases, sides):
        number = len(sides[0])
        shifts = Shifts(bases)
        return [
            taps_queue(
                lhs, shifts, (0, plan.rows), count, dict(enumerate(side)), tiles, (unit,), range(number + tiles - 1)
            )
            for unit, side in enumerate(sides)
        ]

    def keep(into, sides):
        count = into.shape[0]
        for chunk, (left, right) in enumerate(zip(*sides)):
            both = pltpu.matmul_pop(left) + pltpu.matmul_pop(right)
            into[:, chunk * CHUNK : (chunk + 1) * CHUNK] = power(both[:count], both[count:])

    half = chunks // 2

    def halves(accs, sizes):
        each = len(accs) // 2
        groups, at = [], 0
        for size in sizes:
            groups.append([accs[unit * each + at : unit * each + at + size] for unit in (0, 1)])
            at += size
        return groups

    def flat(sides):
        return [acc for side in sides for acc in side]

    for chunk in range(chunks):
        cells[chunk, spread.used :] = jnp.zeros((CHUNK - spread.used, CHUNK), cells.dtype)

    def parts(*accs):
        sides2, sides1, spreads = halves(accs, (number2, number1, half))
        fill_bases(win2, bases2, 0, (plan.part_cols[2] + taps) // LANES)
        fill_bases(win1, bases1, 0, (plan.part_cols[1] + taps) // LANES)
        queues = zip(
            spread.queues(3, plane3, tables, flat(spreads)),
            fill(count2, bases2, sides2),
            fill(count1, bases1, sides1),
        )
        drive([sum(queue, []) for queue in queues])
        spread.drain(3, flat(spreads), cells)
        keep(plane2, sides2)
        keep(plane1, sides1)

    pl.run_scoped(parts, *units([2 * count2] * number2 + [2 * count1] * number1 + [plan.part_rows[3]] * half))

    def total(*accs):
        spreads2, spreads1, sides = halves(accs, (half, half, half))
        totals = [sides[chunk % 2][chunk // 2] for chunk in range(chunks)]
        queues = zip(
            spread.queues(2, plane2, tables, flat(spreads2)),
            spread.queues(1, plane1, tables, flat(spreads1)),
        )
        drive([sum(queue, []) for queue in queues])
        spread.drain(2, flat(spreads2), cells)
        spread.drain(1, flat(spreads1), cells)
        drive(
            [
                [
                    (lambda chunk=chunk: cells[chunk], [(totals[chunk], lambda: pick[...])])
                    for chunk in range(unit, chunks, 2)
                ]
                for unit in (0, 1)
            ]
        )
        for chunk in range(chunks):
            spot = slice(chunk * CHUNK, (chunk + 1) * CHUNK)
            out[:, spot] = plane[:, spot].astype(jnp.float32) + pltpu.matmul_pop(totals[chunk])
            put(chunk).start()

    pl.run_scoped(total, *units([count2] * half + [count1] * half + [plan.rows] * half))
    for chunk in range(chunks):
        put(chunk).wait()


def body(spectrum, template_bank, template_index):
    owners = lax.axis_size("freq")
    taps = template_bank.shape[2]
    rows = template_index.shape[0]
    cols = spectrum.shape[1]
    plan = Plan(cols, taps, rows, owners)
    hbm = pl.BlockSpec(memory_space=pltpu.HBM)
    vmem = pl.BlockSpec(memory_space=pltpu.VMEM)
    wide = [width + taps for width in plan.part_cols]

    def held(*shape, kind=jnp.bfloat16):
        return pltpu.VMEM(shape, kind)

    between = (
        held(rows, cols),
        held(plan.part_rows[3], plan.part_cols[3]),
        held(len(Spread(plan).tables), CHUNK, CHUNK),
        held(rows, CHUNK),
        held(2, wide[1]),
        held(2, wide[2]),
        held(2 * taps // LANES, 2 * rows, LANES),
    )
    inputs = (spectrum, template_index.reshape(1, rows), template_bank)
    results = pl.pallas_call(
        functools.partial(planes_kernel, plan),
        out_shape=between,
        in_specs=[hbm] * 3,
        out_specs=(vmem,) * len(between),
        scratch_shapes=[
            held(2, wide[0]),
            held(2, wide[3]),
            *[held(2, wide[part] // LANES, TILE, LANES) for part in (0, 3)],
            held(taps // LANES, *template_bank.shape[:2], LANES),
            held(1, rows, kind=jnp.int32),
            held(2, plan.granule),
            held(2, max(plan.granule * plan.most, *wide)),
            pltpu.SemaphoreType.DMA((2 + taps // LANES,)),
            pltpu.SemaphoreType.DMA,
            pltpu.SemaphoreType.DMA((len(RATIOS),)),
            pltpu.SemaphoreType.REGULAR,
        ],
        compiler_params=pltpu.CompilerParams(collective_id=0, has_side_effects=True, vmem_limit_bytes=24 * 2**20),
        name="planes",
    )(*[pltpu.with_memory_space_constraint(x, pltpu.HBM) for x in inputs])
    return pl.pallas_call(
        functools.partial(sum_kernel, plan),
        out_shape=jax.ShapeDtypeStruct((rows, cols), jnp.float32),
        in_specs=[vmem] * len(between),
        out_specs=hbm,
        scratch_shapes=[
            held(rows, cols, kind=jnp.float32),
            held(cols // CHUNK, CHUNK, CHUNK),
            *[held(plan.part_rows[part], plan.part_cols[part]) for part in (1, 2)],
            *[held(2, wide[part] // LANES, TILE, LANES) for part in (1, 2)],
            pltpu.SemaphoreType.DMA((cols // CHUNK,)),
        ],
        compiler_params=pltpu.CompilerParams(vmem_limit_bytes=24 * 2**20),
        name="sums",
    )(*results)


def solution(mesh):
    return jax.shard_map(
        body,
        mesh=mesh,
        in_specs=(P(None, ("beam", "freq")), P(), P()),
        out_specs=P(None, ("beam", "freq")),
        check_vma=False,
    )
```
